32 devices in a mesh: event: 8 (over z, x), lon: 4 (over y, core).
Axes of the slice: x: 2, y: 2, z: 4, core: 2. Of those that a mesh axis runs over, the one named last changes fastest.
Arguments:
- adjoint_init: bfloat16 [8, 9, 16, 128, 128], P('event', None, None, 'lon'), may hold values from -6 to 6
- forward_state: bfloat16 [8, 8, 9, 16, 128, 128], P('event', None, None, None, 'lon'), may hold values from -3 to 3
- p_speed: float32 [16, 128, 128], P(None, 'lon'), may hold values from 0.3 to 0.5
- s_speed: float32 [16, 128, 128], P(None, 'lon'), may hold values from 0.1 to 0.2
- density: float32 [16, 128, 128], P(None, 'lon'), may hold values from 0.8 to 1.6
Outputs:
- kernels: float32 [3, 16, 128, 128], P(None, 'event', 'lon')
The draws below stay inside these ranges and needn't reach their ends.
All inputs are finite; a program needn't handle non-finite values.
Results may differ from the reference program's by a relative error of at most 0.015.
Values may be sent and summed in bfloat16 or wider, within the bound.
A program may use at most 64 MiB of HBM per device.

```python
import jax
import jax.numpy as jnp
from jax import lax

LAT = 128
LEV = 16
STEPS = 8
EVENTS = 8
NLON = 128


def raised(values, own_key, source, target, shards_of, factor):
    owner, partner = [(jnp.arange(values.shape[position]) // (values.shape[position] // shards_of)).reshape([-1 if axis == position else 1 for axis in range(values.ndim)]) for position in (source, target)]
    chosen = jax.random.permutation(own_key, shards_of)[partner]
    strong = (owner == chosen) | (owner == (partner + shards_of // 2) % shards_of)
    return jnp.where(strong, factor * values, values)


def shard_levels(stream_key, dims, shards, low, high):
    def one(axis_at, shards_of):
        heights = jax.random.uniform(jax.random.fold_in(jax.random.fold_in(stream_key, 6), axis_at), (shards_of,), jnp.float32, low / len(shards), high / len(shards))
        return jnp.repeat(jnp.exp(heights), dims[axis_at] // shards_of).reshape((-1,) + (1,) * (len(dims) - axis_at - 1))

    loudness = one(*shards[0])
    for cut in shards[1:]:
        loudness = loudness * one(*cut)
    return loudness


def centred(own_key, shape, scale, reach, pieces=(), held_as=jnp.bfloat16):
    factor_of = shard_levels(own_key, shape, pieces, -0.22, 0.18) if pieces else 1.0
    result = jax.random.normal(own_key, shape, jnp.float32) * scale * factor_of
    return jnp.minimum(jnp.maximum(result, -reach), reach).astype(held_as)


def bell_draw_with(own_key, dims, deviation, most, pieces, heavy, dtype=jnp.bfloat16):
    result = deviation * jax.random.normal(own_key, dims, jnp.float32)
    if pieces:
        result = result * shard_levels(own_key, dims, pieces, -0.22, 0.18)
    return jnp.clip(raised(result, jax.random.fold_in(own_key, 3), *heavy), -most, most).astype(dtype)


def setup_inputs(seed: int = 0) -> dict:
    key_list = jax.random.split(jax.random.key(seed), 6)
    return {
        "adjoint_init": centred(key_list[0], (EVENTS, 9, LEV, NLON, LAT), 1.0, 6.0, ((0, 8), (3, 4))),
        "forward_state": bell_draw_with(key_list[1], (EVENTS, STEPS, 9, LEV, NLON, LAT), 0.5, 3.0, ((0, 8), (4, 4)), (0, 3, 8, 2.0)),
        "p_speed": jnp.clip(0.3 + 0.19999999 * jax.random.uniform(key_list[2], (LEV, NLON, LAT), jnp.float32) ** shard_levels(key_list[2], (LEV, NLON, LAT), ((1, 4),), -0.2, 0.2), 0.3, 0.5),
        "s_speed": jnp.clip(0.1 + 0.1 * jax.random.uniform(key_list[3], (LEV, NLON, LAT), jnp.float32) ** shard_levels(key_list[3], (LEV, NLON, LAT), ((1, 4),), -0.2, 0.2), 0.1, 0.2),
        "density": jnp.clip(0.8 + 0.8 * jax.random.uniform(key_list[4], (LEV, NLON, LAT), jnp.float32) ** shard_levels(key_list[4], (LEV, NLON, LAT), ((1, 4),), -0.2, 0.2), 0.8, 1.6),
    }


def ahead_diff(values, along):
    length = values.shape[along]
    border = jnp.zeros_like(lax.slice_in_dim(values, 0, 1, axis=along))
    return jnp.concatenate([lax.slice_in_dim(values, 1, length, axis=along), border], axis=along) - values


def behind_diff(values, along):
    length = values.shape[along]
    border = jnp.zeros_like(lax.slice_in_dim(values, 0, 1, axis=along))
    return values - jnp.concatenate([border, lax.slice_in_dim(values, 0, length - 1, axis=along)], axis=along)


def cycle_ahead(values, along):
    return jnp.roll(values, -1, axis=along) - values


def cycle_behind(values, along):
    return values - jnp.roll(values, 1, axis=along)


def forcing(stress, lon_ahead, lon_behind):
    stress_xx, stress_yy, stress_zz, stress_xy, stress_xz, stress_yz = [stress[index].astype(jnp.float32) for index in range(6)]
    force_x = lon_ahead(stress_xx, 1) + behind_diff(stress_xy, 2) + behind_diff(stress_xz, 0)
    force_y = lon_behind(stress_xy, 1) + ahead_diff(stress_yy, 2) + behind_diff(stress_yz, 0)
    force_z = lon_behind(stress_xz, 1) + behind_diff(stress_yz, 2) + ahead_diff(stress_zz, 0)
    return force_x, force_y, force_z


def strain_rates(velocity, lon_ahead, lon_behind):
    speed_x, speed_y, speed_z = [velocity[index].astype(jnp.float32) for index in range(3)]
    rate_xx = lon_behind(speed_x, 1)
    rate_yy = behind_diff(speed_y, 2)
    rate_zz = behind_diff(speed_z, 0)
    rate_xy = 0.5 * (ahead_diff(speed_x, 2) + lon_ahead(speed_y, 1))
    rate_xz = 0.5 * (ahead_diff(speed_x, 0) + lon_ahead(speed_z, 1))
    rate_yz = 0.5 * (ahead_diff(speed_y, 0) + ahead_diff(speed_z, 2))
    return rate_xx, rate_yy, rate_zz, rate_xy, rate_xz, rate_yz


def update_stress(stress, strain_rate, lame_coef, shear_coef):
    rate_xx, rate_yy, rate_zz, rate_xy, rate_xz, rate_yz = strain_rate
    trace_rate = rate_xx + rate_yy + rate_zz
    twice_shear = 2.0 * shear_coef
    volume_part = lame_coef * trace_rate
    updated = [
        stress[0].astype(jnp.float32) + volume_part + twice_shear * rate_xx,
        stress[1].astype(jnp.float32) + volume_part + twice_shear * rate_yy,
        stress[2].astype(jnp.float32) + volume_part + twice_shear * rate_zz,
        stress[3].astype(jnp.float32) + twice_shear * rate_xy,
        stress[4].astype(jnp.float32) + twice_shear * rate_xz,
        stress[5].astype(jnp.float32) + twice_shear * rate_yz,
    ]
    return jnp.stack([item.astype(jnp.bfloat16) for item in updated])


def kernel_terms(velocity, strain_rate, forward_now):
    rate_xx, rate_yy, rate_zz, rate_xy, rate_xz, rate_yz = strain_rate
    forward_f = [forward_now[index].astype(jnp.float32) for index in range(9)]
    trace_rate = rate_xx + rate_yy + rate_zz
    lame_term = trace_rate * (forward_f[3] + forward_f[4] + forward_f[5])
    shear_term = 2.0 * (rate_xx * forward_f[3] + rate_yy * forward_f[4] + rate_zz * forward_f[5]
                        + 2.0 * (rate_xy * forward_f[6] + rate_xz * forward_f[7] + rate_yz * forward_f[8]))
    speed = [velocity[index].astype(jnp.float32) for index in range(3)]
    density_term = speed[0] * forward_f[0] + speed[1] * forward_f[1] + speed[2] * forward_f[2]
    return lame_term, shear_term, density_term


def combine_kernels(kernel_total, p_speed, s_speed, density):
    lame_coef = density * (p_speed * p_speed - 2.0 * s_speed * s_speed)
    shear_coef = density * s_speed * s_speed
    return jnp.stack([
        2.0 * density * p_speed * p_speed * kernel_total[0],
        2.0 * density * s_speed * s_speed * (kernel_total[1] - 2.0 * kernel_total[0]),
        density * kernel_total[2] + lame_coef * kernel_total[0] + shear_coef * kernel_total[1],
    ])


def reference(adjoint_init, forward_state, p_speed, s_speed, density):
    lame_coef = density * (p_speed * p_speed - 2.0 * s_speed * s_speed)
    shear_coef = density * s_speed * s_speed
    buoyancy = 1.0 / density

    def advance(state_pair, forward_now):
        fields, kernel_sums = state_pair
        force = forcing(fields[3:9], cycle_ahead, cycle_behind)
        velocity = jnp.stack([(fields[index].astype(jnp.float32) + buoyancy * force[index]).astype(jnp.bfloat16) for index in range(3)])
        strain_rate = strain_rates(velocity, cycle_ahead, cycle_behind)
        stress = update_stress(fields[3:9], strain_rate, lame_coef, shear_coef)
        kernel_sums = kernel_sums + jnp.stack(kernel_terms(velocity, strain_rate, forward_now))
        return (jnp.concatenate([velocity, stress]), kernel_sums), None

    def per_event(event_total, event_inputs):
        initial, forward = event_inputs
        blank_sums = jnp.zeros((3,) + p_speed.shape, jnp.float32)
        (final_fields, kernel_sums), unused = lax.scan(advance, (initial, blank_sums), forward)
        return event_total + kernel_sums, None

    kernel_total, unused = lax.scan(per_event, jnp.zeros((3,) + p_speed.shape, jnp.float32), (adjoint_init, forward_state))
    return combine_kernels(kernel_total, p_speed, s_speed, density)
```

```python
import jax
import jax.numpy as jnp
from jax import lax
from jax.experimental import pallas as pl
from jax.experimental.pallas import tpu as pltpu
from jax.sharding import PartitionSpec as P

XX, YY, ZZ, XY, XZ, YZ = range(6)
VX, VY, VZ = range(3)
BUOY, LAME, SHEAR, TWICE = range(4)
TILE = 8
MESH = pl.DeviceIdType.MESH


def behind_lat(a):
    lane = lax.broadcasted_iota(jnp.int32, a.shape, 1)
    return a - jnp.where(lane == 0, 0.0, pltpu.roll(a, 1, 1))


def ahead_lat(a):
    lane = lax.broadcasted_iota(jnp.int32, a.shape, 1)
    last = a.shape[1] - 1
    return jnp.where(lane == last, 0.0, pltpu.roll(a, last, 1)) - a


def kernel(
    adj_hbm, fwd_hbm, p_hbm, s_hbm, d_hbm, out_ref,
    adj, fwd, p_raw, s_raw, d_raw,
    v_even, v_odd, s_even, s_odd, mat,
    halo_out, halo_in, mid_out, mid_in, edge_out, edge_in,
    local_sem, fwd_sem, halo_send, halo_recv, red_send, red_recv, lon_sem, all_sem,
):
    levels, own, lat = p_raw.shape
    steps = fwd.shape[0]
    halo = steps
    events, ring = lax.axis_size("event"), lax.axis_size("lon")
    me_e, me_l = lax.axis_index("event"), lax.axis_index("lon")
    right, left = lax.rem(me_l + 1, ring), lax.rem(me_l + ring - 1, ring)
    share = levels // events
    odd = lax.rem(me_l, 2)
    first_side = 1 - odd

    def peer(d):
        return (lax.rem(me_e + d, events), me_l)

    local = [
        pltpu.make_async_copy(src, dst, local_sem.at[k])
        for k, (src, dst) in enumerate(
            ((adj_hbm.at[0], adj), (d_hbm, d_raw), (p_hbm, p_raw), (s_hbm, s_raw))
        )
    ]
    for copy in local:
        copy.start()

    def fwd_copy(t):
        return pltpu.make_async_copy(fwd_hbm.at[0, t], fwd.at[t], fwd_sem.at[t])

    for t in range(steps):
        fwd_copy(t).start()

    barrier = pltpu.get_barrier_semaphore()

    @pl.when(odd == 1)
    def _():
        for neighbour in (left, right):
            pl.semaphore_signal(barrier, inc=1, device_id=(me_e, neighbour), device_id_type=MESH)

    zeros = jnp.zeros((own + 2 * halo, lat), jnp.float32)
    for ref, count in ((v_even, steps // 2 + 1), (v_odd, steps // 2)):
        for i in range(count):
            ref[i, VZ, 0] = zeros
            ref[i, VX, levels + 1] = zeros
            ref[i, VY, levels + 1] = zeros

    for copy in local:
        copy.wait()

    def prepare(i, carry):
        edges = [[[], []] for _ in range(12)]
        for j in range(2):
            z = 2 * i + j
            d, p, s = d_raw[z], p_raw[z], s_raw[z]
            shear = d * s * s
            rows = [adj[f, z].astype(jnp.float32) for f in range(9)]
            rows += [1.0 / d, d * (p * p - 2.0 * s * s), shear]
            for f in range(3):
                v_even[0, f, z + 1, halo:halo + own, :] = rows[f]
            for f in range(6):
                s_even[f, z, halo:halo + own, :] = rows[3 + f]
            for f in range(3):
                mat[f, z, halo:halo + own, :] = rows[9 + f]
            mat[TWICE, z, halo:halo + own, :] = shear + shear
            for f in range(12):
                edges[f][0].append(rows[f][:halo])
                edges[f][1].append(rows[f][own - halo:])
        for f in range(12):
            for side in range(2):
                pair = jnp.concatenate(edges[f][side], axis=0)
                halo_out[side, f, i] = pair.astype(jnp.bfloat16)
        return carry

    lax.fori_loop(0, levels // 2, prepare, 0)

    @pl.when(odd == 0)
    def _():
        pl.semaphore_wait(barrier, 2)
        for neighbour in (left, right):
            pl.semaphore_signal(lon_sem, inc=1, device_id=(me_e, neighbour), device_id_type=MESH)

    @pl.when(odd == 1)
    def _():
        pl.semaphore_wait(lon_sem, 2)
        for d in range(1, events):
            pl.semaphore_signal(barrier, inc=1, device_id=peer(d), device_id_type=MESH)

    def exchange(side):
        return pltpu.make_async_remote_copy(
            src_ref=halo_out.at[side], dst_ref=halo_in.at[side],
            send_sem=halo_send.at[side], recv_sem=halo_recv.at[side],
            device_id=(me_e, jnp.where(side == 0, left, right)), device_id_type=MESH,
        )

    for side in range(2):
        exchange(side).start()

    def receive(side):
        source = 1 - side
        exchange(source).wait_recv()
        start = jnp.where(side == 0, 0, halo + own)

        def unpack(i, carry):
            for f in range(12):
                pair = halo_in[source, f, i].astype(jnp.float32)
                for j in range(2):
                    rows = pair[j * halo:(j + 1) * halo]
                    z = 2 * i + j
                    if f < 3:
                        v_even[0, f, z + 1, pl.ds(start, halo), :] = rows
                    elif f < 9:
                        s_even[f - 3, z, pl.ds(start, halo), :] = rows
                    else:
                        mat[f - 9, z, pl.ds(start, halo), :] = rows
                        if f - 9 == SHEAR:
                            mat[TWICE, z, pl.ds(start, halo), :] = rows + rows
            return carry

        lax.fori_loop(0, levels // 2, unpack, 0)

    def velocity(s_ref, v_from, i_from, v_to, i_to, q):
        base = halo + q
        here, back = pl.ds(base, TILE), pl.ds(base - 1, TILE)
        for z in range(levels):
            if z == 0:
                xz_under = yz_under = None
                zz = s_ref[ZZ, 0, here, :]
            xy, xy_back = s_ref[XY, z, here, :], s_ref[XY, z, back, :]
            xz, xz_back = s_ref[XZ, z, here, :], s_ref[XZ, z, back, :]
            yz = s_ref[YZ, z, here, :]
            fx = (s_ref[XX, z, here, :] - s_ref[XX, z, back, :]) + behind_lat(xy_back)
            fy = (xy - xy_back) + ahead_lat(s_ref[YY, z, here, :])
            fz = (xz - xz_back) + behind_lat(yz)
            fx = fx + (xz_back if z == 0 else xz_back - xz_under)
            fy = fy + (yz if z == 0 else yz - yz_under)
            xz_under, yz_under = xz_back, yz
            if z + 1 < levels:
                above = s_ref[ZZ, z + 1, here, :]
                fz = fz + (above - zz)
                zz = above
            else:
                fz = fz - zz
            b, b_back = mat[BUOY, z, here, :], mat[BUOY, z, back, :]
            v_to[i_to, VX, z + 1, back, :] = v_from[i_from, VX, z + 1, back, :] + b_back * fx
            v_to[i_to, VY, z + 1, here, :] = v_from[i_from, VY, z + 1, here, :] + b * fy
            v_to[i_to, VZ, z + 1, here, :] = v_from[i_from, VZ, z + 1, here, :] + b * fz

    def stress(s_from, s_to, v_ref, i_v, q):
        base = halo + q
        here, back, ahead = (pl.ds(base + k, TILE) for k in (0, -1, 1))
        for z in range(levels):
            if z == 0:
                vx, vy, vz_under = v_ref[i_v, VX, 1, here, :], v_ref[i_v, VY, 1, here, :], None
            vz = v_ref[i_v, VZ, z + 1, here, :]
            exx = vx - v_ref[i_v, VX, z + 1, back, :]
            eyy = behind_lat(vy)
            ezz = vz if z == 0 else vz - vz_under
            gxy = ahead_lat(vx) + (v_ref[i_v, VY, z + 1, ahead, :] - vy)
            gxz = v_ref[i_v, VZ, z + 1, ahead, :] - vz
            gyz = ahead_lat(vz)
            vz_under = vz
            if z + 1 < levels:
                above_x, above_y = v_ref[i_v, VX, z + 2, here, :], v_ref[i_v, VY, z + 2, here, :]
                gxz, gyz = gxz + (above_x - vx), gyz + (above_y - vy)
                vx, vy = above_x, above_y
            else:
                gxz, gyz = gxz - vx, gyz - vy
            volume = mat[LAME, z, here, :] * (exx + eyy + ezz)
            twice, shear = mat[TWICE, z, here, :], mat[SHEAR, z, here, :]
            for f, e in ((XX, exx), (YY, eyy), (ZZ, ezz)):
                s_to[f, z, here, :] = (s_from[f, z, here, :] + volume) + twice * e
            for f, g in ((XY, gxy), (XZ, gxz), (YZ, gyz)):
                s_to[f, z, here, :] = s_from[f, z, here, :] + shear * g

    def advance(phase, side):
        inner = phase == 0

        def pair(i, carry):
            for parity in range(2):
                t = 2 * i + 1 + parity
                s_from, s_to = (s_even, s_odd) if parity == 0 else (s_odd, s_even)
                v_from, v_to = (v_even, v_odd) if parity == 0 else (v_odd, v_even)

                def v_block(b, carry, s_from=s_from, v_from=v_from, v_to=v_to, t=t, up=parity):
                    edge = jnp.where(side == 0, t - halo, own + 1 - t)
                    q = jnp.where(inner, jnp.minimum(t + TILE * b, own - TILE + 1 - t), edge)
                    velocity(s_from, v_from, i, v_to, i + up, q)
                    return carry

                def s_block(b, carry, s_from=s_from, s_to=s_to, v_to=v_to, t=t, up=parity):
                    edge = jnp.where(side == 0, t - halo, own - t)
                    q = jnp.where(inner, jnp.minimum(t + TILE * b, own - TILE - t), edge)
                    stress(s_from, s_to, v_to, i + up, q)
                    return carry

                blocks = jnp.where(inner, (own + 1 - 2 * t + TILE - 1) // TILE, 1)
                lax.fori_loop(0, blocks, v_block, 0)
                blocks = jnp.where(inner, (own - 2 * t + TILE - 1) // TILE, 1)
                blocks = jnp.where(t < steps, blocks, 0)
                lax.fori_loop(0, blocks, s_block, 0)
            return carry

        lax.fori_loop(0, steps // 2, pair, 0)

    def sums(owner, start, n, rows_of):
        totals = [[None] * 3 for _ in range(share)]
        rows = slice(halo + start, halo + start + n)
        for t in range(1, steps + 1):
            v_ref, i = (v_odd, (t - 1) // 2) if t % 2 else (v_even, t // 2)
            for j in range(share):
                z = owner * share + j

                def v(c, off=0, dz=0):
                    return v_ref[i, c, z + 1 + dz, rows.start + off:rows.stop + off, :]

                if j == 0:
                    vx, vy, under = v(VX), v(VY), v(VZ, 0, -1)
                vz, above_x, above_y = v(VZ), v(VX, 0, 1), v(VY, 0, 1)
                F = [rows_of(t - 1, f, z) for f in range(9)]
                exx = vx - v(VX, -1)
                eyy = behind_lat(vy)
                ezz = vz - under
                gxy = ahead_lat(vx) + (v(VY, 1) - vy)
                gxz = (above_x - vx) + (v(VZ, 1) - vz)
                gyz = (above_y - vy) + ahead_lat(vz)
                terms = (
                    (exx + eyy + ezz) * (F[3] + F[4] + F[5]),
                    (exx * F[3] + eyy * F[4] + ezz * F[5]) + (gxy * F[6] + gxz * F[7] + gyz * F[8]),
                    vx * F[0] + vy * F[1] + vz * F[2],
                )
                vx, vy, under = above_x, above_y, vz
                for k in range(3):
                    old = totals[j][k]
                    totals[j][k] = terms[k] if old is None else old + terms[k]
        return totals

    def red_copy(kind, d):
        src, dst = (mid_out, mid_in) if kind == 0 else (edge_out.at[kind - 1], edge_in.at[kind - 1])
        return pltpu.make_async_remote_copy(
            src_ref=src.at[d], dst_ref=dst.at[d],
            send_sem=red_send.at[kind, d], recv_sem=red_recv.at[kind, d],
            device_id=peer(d), device_id_type=MESH,
        )

    def send(kind, d):
        @pl.when(d != 0)
        def _():
            red_copy(kind, d).start()

    def mid_sums():
        first, count = halo, own - 2 * halo

        def one(k, carry):
            d = lax.rem(k + 1, events)
            owner = lax.rem(me_e + d, events)
            totals = sums(
                owner, first, count,
                lambda t, f, z: fwd[t, f, z, :, :].astype(jnp.float32)[first:first + count],
            )
            for j in range(share):
                for i in range(3):
                    mid_out[d, i * share + j] = totals[j][i].astype(jnp.bfloat16)
            send(0, d)
            return carry

        lax.fori_loop(0, events, one, 0)

    def edge_sums(side):
        start = 0 if side == 0 else own - halo
        group = 0 if side == 0 else own - 2 * TILE

        def one(k, carry):
            d = lax.rem(k + 1, events)
            owner = lax.rem(me_e + d, events)
            totals = sums(
                owner, start, halo,
                lambda t, f, z: fwd[t, f, z, group:group + 2 * TILE, :].astype(jnp.float32)[
                    start - group:start - group + halo
                ],
            )
            flat = [totals[j][i] for i in range(3) for j in range(share)]
            if len(flat) % 2:
                flat.append(flat[-1])
            for m in range(len(flat) // 2):
                pair = jnp.concatenate(flat[2 * m:2 * m + 2], axis=0)
                edge_out[side, d, m] = pair.astype(jnp.bfloat16)
            send(1 + side, d)
            return carry

        lax.fori_loop(0, events, one, 0)

    def phases(phase, carry):
        side = jnp.where(phase == 1, first_side, 1 - first_side)

        @pl.when(phase > 0)
        def _():
            receive(side)

        advance(phase, side)

        @pl.when(phase == 0)
        def _():
            @pl.when(odd == 1)
            def _():
                pl.semaphore_wait(barrier, events - 1)
                pl.semaphore_signal(all_sem, inc=1, device_id=(me_e, left), device_id_type=MESH)

            @pl.when(odd == 0)
            def _():
                pl.semaphore_wait(all_sem, 1)

            for t in range(steps):
                fwd_copy(t).wait()
            mid_sums()

        for value in range(2):
            @pl.when((phase > 0) & (side == value))
            def _():
                edge_sums(value)

        return carry

    lax.fori_loop(0, 3, phases, 0)

    def combine(j, start, n, totals):
        k_lame, half_shear, k_dens = totals
        k_shear = 2.0 * half_shear
        z = me_e * share + j
        p, s, d = (x[z, start:start + n, :] for x in (p_raw, s_raw, d_raw))
        lame, shear = d * (p * p - 2.0 * s * s), d * s * s
        out_ref[0, j, start:start + n, :] = 2.0 * d * p * p * k_lame
        out_ref[1, j, start:start + n, :] = 2.0 * d * s * s * (k_shear - 2.0 * k_lame)
        out_ref[2, j, start:start + n, :] = d * k_dens + lame * k_lame + shear * k_shear

    def gathered(out, into, m):
        return out[0, m].astype(jnp.float32) + sum(
            into[d, m].astype(jnp.float32) for d in range(1, events)
        )

    for d in range(1, events):
        red_copy(0, d).wait()
    for j in range(share):
        combine(
            j, halo, own - 2 * halo, [gathered(mid_out, mid_in, i * share + j) for i in range(3)]
        )

    for side in range(2):
        exchange(side).wait_send()

    for side in range(2):
        for d in range(1, events):
            red_copy(1 + side, d).wait()
    for side in range(2):
        start = 0 if side == 0 else own - halo
        tiles = [gathered(edge_out.at[side], edge_in.at[side], m) for m in range(edge_out.shape[2])]
        flat = [t[h * halo:(h + 1) * halo] for t in tiles for h in range(2)]
        for j in range(share):
            combine(j, start, halo, [flat[i * share + j] for i in range(3)])


def shards(adjoint_init, forward_state, p_speed, s_speed, density):
    levels, own, lat = p_speed.shape
    steps = forward_state.shape[1]
    events = lax.axis_size("event")
    share, halo = levels // events, steps
    assert halo == TILE and own % 16 == 0 and own >= 4 * TILE and lax.axis_size("lon") % 2 == 0
    rows = own + 2 * halo
    f32, bf16 = jnp.float32, jnp.bfloat16
    anywhere = pl.BlockSpec(memory_space=pltpu.HBM)
    edge_tiles = (3 * share + 1) // 2
    dma = pltpu.SemaphoreType.DMA
    return pl.pallas_call(
        kernel,
        out_shape=jax.ShapeDtypeStruct((3, share, own, lat), f32),
        in_specs=[anywhere] * 5,
        out_specs=pl.BlockSpec(memory_space=pltpu.VMEM),
        scratch_shapes=[
            pltpu.VMEM(adjoint_init.shape[1:], bf16),
            pltpu.VMEM(forward_state.shape[1:], bf16),
            pltpu.VMEM(p_speed.shape, f32),
            pltpu.VMEM(p_speed.shape, f32),
            pltpu.VMEM(p_speed.shape, f32),
            pltpu.VMEM((steps // 2 + 1, 3, levels + 2, rows, lat), f32),
            pltpu.VMEM((steps // 2, 3, levels + 2, rows, lat), f32),
            pltpu.VMEM((6, levels, rows, lat), f32),
            pltpu.VMEM((6, levels, rows, lat), f32),
            pltpu.VMEM((4, levels, rows, lat), f32),
            pltpu.VMEM((2, 12, levels // 2, 2 * halo, lat), bf16),
            pltpu.VMEM((2, 12, levels // 2, 2 * halo, lat), bf16),
            pltpu.VMEM((events, 3 * share, own - 2 * halo, lat), bf16),
            pltpu.VMEM((events, 3 * share, own - 2 * halo, lat), bf16),
            pltpu.VMEM((2, events, edge_tiles, 2 * halo, lat), bf16),
            pltpu.VMEM((2, events, edge_tiles, 2 * halo, lat), bf16),
            dma((4,)), dma((steps,)), dma((2,)), dma((2,)),
            dma((3, events)), dma((3, events)),
            pltpu.SemaphoreType.REGULAR, pltpu.SemaphoreType.REGULAR,
        ],
        compiler_params=pltpu.CompilerParams(
            collective_id=0, has_side_effects=True, vmem_limit_bytes=60 * 2**20
        ),
        name="adjoint",
    )(adjoint_init, forward_state, p_speed, s_speed, density)


def solution(mesh):
    placed = (
        P("event", None, None, "lon", None),
        P("event", None, None, None, "lon", None),
        P(None, "lon", None),
        P(None, "lon", None),
        P(None, "lon", None),
    )
    return jax.shard_map(
        shards, mesh=mesh, in_specs=placed, out_specs=P(None, "event", "lon", None), check_vma=False
    )
```

```python
import jax
import jax.numpy as jnp
from jax import lax
from jax.experimental import pallas as pl
from jax.experimental.pallas import tpu as pltpu
from jax.sharding import PartitionSpec as P

XX, YY, ZZ, XY, XZ, YZ = range(6)
VX, VY, VZ = range(3)
BUOY, LAME, SHEAR, TWICE = range(4)
TILE = 8
MESH = pl.DeviceIdType.MESH


def behind_lat(a):
    lane = lax.broadcasted_iota(jnp.int32, a.shape, 1)
    return a - jnp.where(lane == 0, 0.0, pltpu.roll(a, 1, 1))


def ahead_lat(a):
    lane = lax.broadcasted_iota(jnp.int32, a.shape, 1)
    last = a.shape[1] - 1
    return jnp.where(lane == last, 0.0, pltpu.roll(a, last, 1)) - a


def kernel(
    adj_hbm, fwd_hbm, p_hbm, s_hbm, d_hbm, out_ref,
    adj, fwd, p_raw, s_raw, d_raw,
    v_even, v_odd, s_even, s_odd, rates, mat,
    halo_out, halo_in, mid_out, mid_in, edge_out, edge_in,
    local_sem, fwd_sem, halo_send, halo_recv, red_send, red_recv, lon_sem, all_sem,
):
    levels, own, lat = p_raw.shape
    steps = fwd.shape[0]
    halo = steps
    events, ring = lax.axis_size("event"), lax.axis_size("lon")
    me_e, me_l = lax.axis_index("event"), lax.axis_index("lon")
    right, left = lax.rem(me_l + 1, ring), lax.rem(me_l + ring - 1, ring)
    share = levels // events
    odd = lax.rem(me_l, 2)
    first_side = 1 - odd

    def peer(d):
        return (lax.rem(me_e + d, events), me_l)

    local = [
        pltpu.make_async_copy(src, dst, local_sem.at[k])
        for k, (src, dst) in enumerate(
            ((adj_hbm.at[0], adj), (d_hbm, d_raw), (p_hbm, p_raw), (s_hbm, s_raw))
        )
    ]
    for copy in local:
        copy.start()

    def fwd_copy(t):
        return pltpu.make_async_copy(fwd_hbm.at[0, t], fwd.at[t], fwd_sem.at[t])

    barrier = pltpu.get_barrier_semaphore()

    @pl.when(odd == 1)
    def _():
        for neighbour in (left, right):
            pl.semaphore_signal(barrier, inc=1, device_id=(me_e, neighbour), device_id_type=MESH)

    zeros = jnp.zeros((own + 2 * halo, lat), jnp.float32)
    for ref, count in ((v_even, steps // 2 + 1), (v_odd, steps // 2)):
        for i in range(count):
            ref[i, VZ, 0] = zeros
            ref[i, VX, levels + 1] = zeros
            ref[i, VY, levels + 1] = zeros

    for copy in local:
        copy.wait()
    for t in range(steps):
        fwd_copy(t).start()

    def prepare(i, carry):
        edges = [[[], []] for _ in range(12)]
        for j in range(2):
            z = 2 * i + j
            d, p, s = d_raw[z], p_raw[z], s_raw[z]
            shear = d * s * s
            rows = [adj[f, z].astype(jnp.float32) for f in range(9)]
            rows += [1.0 / d, d * (p * p - 2.0 * s * s), shear]
            for f in range(3):
                v_even[0, f, z + 1, halo:halo + own, :] = rows[f]
            for f in range(6):
                s_even[f, z, halo:halo + own, :] = rows[3 + f]
            for f in range(3):
                mat[f, z, halo:halo + own, :] = rows[9 + f]
            mat[TWICE, z, halo:halo + own, :] = shear + shear
            for f in range(12):
                edges[f][0].append(rows[f][:halo])
                edges[f][1].append(rows[f][own - halo:])
        for f in range(12):
            for side in range(2):
                pair = jnp.concatenate(edges[f][side], axis=0)
                halo_out[side, f, i] = pair.astype(jnp.bfloat16)
        return carry

    lax.fori_loop(0, levels // 2, prepare, 0)

    def exchange(side):
        return pltpu.make_async_remote_copy(
            src_ref=halo_out.at[side], dst_ref=halo_in.at[side],
            send_sem=halo_send.at[side], recv_sem=halo_recv.at[side],
            device_id=(me_e, jnp.where(side == 0, left, right)), device_id_type=MESH,
        )

    def start_exchange():
        for side in range(2):
            exchange(side).start()

    def answer():
        pl.semaphore_wait(barrier, 2)
        for neighbour in (left, right):
            pl.semaphore_signal(lon_sem, inc=1, device_id=(me_e, neighbour), device_id_type=MESH)
        start_exchange()

    def greet_events():
        pl.semaphore_wait(lon_sem, 2)
        start_exchange()
        for d in range(1, events):
            pl.semaphore_signal(barrier, inc=1, device_id=peer(d), device_id_type=MESH)

    def receive(side):
        source = 1 - side
        exchange(source).wait_recv()
        start = jnp.where(side == 0, 0, halo + own)

        def unpack(i, carry):
            for f in range(12):
                pair = halo_in[source, f, i].astype(jnp.float32)
                for j in range(2):
                    rows = pair[j * halo:(j + 1) * halo]
                    z = 2 * i + j
                    if f < 3:
                        v_even[0, f, z + 1, pl.ds(start, halo), :] = rows
                    elif f < 9:
                        s_even[f - 3, z, pl.ds(start, halo), :] = rows
                    else:
                        mat[f - 9, z, pl.ds(start, halo), :] = rows
                        if f - 9 == SHEAR:
                            mat[TWICE, z, pl.ds(start, halo), :] = rows + rows
            return carry

        lax.fori_loop(0, levels // 2, unpack, 0)

    def velocity(s_ref, v_from, i_from, v_to, i_to, q):
        base = halo + q
        here, back = pl.ds(base, TILE), pl.ds(base - 1, TILE)
        for z in range(levels):
            if z == 0:
                xz_under = yz_under = None
                zz = s_ref[ZZ, 0, here, :]
            xy, xy_back = s_ref[XY, z, here, :], s_ref[XY, z, back, :]
            xz, xz_back = s_ref[XZ, z, here, :], s_ref[XZ, z, back, :]
            yz = s_ref[YZ, z, here, :]
            fx = (s_ref[XX, z, here, :] - s_ref[XX, z, back, :]) + behind_lat(xy_back)
            fy = (xy - xy_back) + ahead_lat(s_ref[YY, z, here, :])
            fz = (xz - xz_back) + behind_lat(yz)
            fx = fx + (xz_back if z == 0 else xz_back - xz_under)
            fy = fy + (yz if z == 0 else yz - yz_under)
            xz_under, yz_under = xz_back, yz
            if z + 1 < levels:
                above = s_ref[ZZ, z + 1, here, :]
                fz = fz + (above - zz)
                zz = above
            else:
                fz = fz - zz
            b, b_back = mat[BUOY, z, here, :], mat[BUOY, z, back, :]
            v_to[i_to, VX, z + 1, back, :] = v_from[i_from, VX, z + 1, back, :] + b_back * fx
            v_to[i_to, VY, z + 1, here, :] = v_from[i_from, VY, z + 1, here, :] + b * fy
            v_to[i_to, VZ, z + 1, here, :] = v_from[i_from, VZ, z + 1, here, :] + b * fz

    def stress(s_from, s_to, v_ref, i_v, e_at, q):
        base = halo + q
        here, back, ahead = (pl.ds(base + k, TILE) for k in (0, -1, 1))
        for z in range(levels):
            if z == 0:
                vx, vy, vz_under = v_ref[i_v, VX, 1, here, :], v_ref[i_v, VY, 1, here, :], None
            vz = v_ref[i_v, VZ, z + 1, here, :]
            exx = vx - v_ref[i_v, VX, z + 1, back, :]
            eyy = behind_lat(vy)
            ezz = vz if z == 0 else vz - vz_under
            gxy = ahead_lat(vx) + (v_ref[i_v, VY, z + 1, ahead, :] - vy)
            gxz = v_ref[i_v, VZ, z + 1, ahead, :] - vz
            gyz = ahead_lat(vz)
            vz_under = vz
            if z + 1 < levels:
                above_x, above_y = v_ref[i_v, VX, z + 2, here, :], v_ref[i_v, VY, z + 2, here, :]
                gxz, gyz = gxz + (above_x - vx), gyz + (above_y - vy)
                vx, vy = above_x, above_y
            else:
                gxz, gyz = gxz - vx, gyz - vy
            for f, e in enumerate((exx, eyy, ezz, gxy, gxz, gyz)):
                rates[e_at, f, z, here, :] = e
            volume = mat[LAME, z, here, :] * (exx + eyy + ezz)
            twice, shear = mat[TWICE, z, here, :], mat[SHEAR, z, here, :]
            for f, e in ((XX, exx), (YY, eyy), (ZZ, ezz)):
                s_to[f, z, here, :] = (s_from[f, z, here, :] + volume) + twice * e
            for f, g in ((XY, gxy), (XZ, gxz), (YZ, gyz)):
                s_to[f, z, here, :] = s_from[f, z, here, :] + shear * g

    def advance(phase, side):
        inner = phase == 0

        def pair(i, carry):
            for parity in range(2):
                t = 2 * i + 1 + parity
                s_from, s_to = (s_even, s_odd) if parity == 0 else (s_odd, s_even)
                v_from, v_to = (v_even, v_odd) if parity == 0 else (v_odd, v_even)

                def v_block(b, carry, s_from=s_from, v_from=v_from, v_to=v_to, t=t, up=parity):
                    edge = jnp.where(side == 0, t - halo, own + 1 - t)
                    q = jnp.where(inner, jnp.minimum(t + TILE * b, own - TILE + 1 - t), edge)
                    velocity(s_from, v_from, i, v_to, i + up, q)
                    return carry

                def s_block(b, carry, s_from=s_from, s_to=s_to, v_to=v_to, t=t, up=parity):
                    edge = jnp.where(side == 0, t - halo, own - t)
                    q = jnp.where(inner, jnp.minimum(t + TILE * b, own - TILE - t), edge)
                    stress(s_from, s_to, v_to, i + up, t - 1, q)
                    return carry

                blocks = jnp.where(inner, (own + 1 - 2 * t + TILE - 1) // TILE, 1)
                lax.fori_loop(0, blocks, v_block, 0)
                blocks = jnp.where(inner, (own - 2 * t + TILE - 1) // TILE, 1)
                blocks = jnp.where(t < steps, blocks, 0)
                lax.fori_loop(0, blocks, s_block, 0)

                @pl.when(inner & (i == 0) & (odd == parity))
                def _(parity=parity):
                    answer() if parity == 0 else greet_events()
            return carry

        lax.fori_loop(0, steps // 2, pair, 0)

    def sums(owner, start, n, rows_of):
        totals = [[None] * 3 for _ in range(share)]
        rows = slice(halo + start, halo + start + n)
        for t in range(1, steps + 1):
            v_ref, i = (v_odd, (t - 1) // 2) if t % 2 else (v_even, t // 2)
            for j in range(share):
                z = owner * share + j

                def v(c, off=0, dz=0):
                    return v_ref[i, c, z + 1 + dz, rows.start + off:rows.stop + off, :]

                F = [rows_of(t - 1, f, z) for f in range(9)]
                if t < steps:
                    vx, vy, vz = v(VX), v(VY), v(VZ)
                    exx, eyy, ezz, gxy, gxz, gyz = (rates[t - 1, f, z, rows, :] for f in range(6))
                else:
                    if j == 0:
                        vx, vy, under = v(VX), v(VY), v(VZ, 0, -1)
                    else:
                        vx, vy, under = above_x, above_y, vz
                    vz, above_x, above_y = v(VZ), v(VX, 0, 1), v(VY, 0, 1)
                    exx = vx - v(VX, -1)
                    eyy = behind_lat(vy)
                    ezz = vz - under
                    gxy = ahead_lat(vx) + (v(VY, 1) - vy)
                    gxz = (above_x - vx) + (v(VZ, 1) - vz)
                    gyz = (above_y - vy) + ahead_lat(vz)
                terms = (
                    (exx + eyy + ezz) * (F[3] + F[4] + F[5]),
                    (exx * F[3] + eyy * F[4] + ezz * F[5]) + (gxy * F[6] + gxz * F[7] + gyz * F[8]),
                    vx * F[0] + vy * F[1] + vz * F[2],
                )
                for k in range(3):
                    old = totals[j][k]
                    totals[j][k] = terms[k] if old is None else old + terms[k]
        return totals

    def red_copy(kind, d):
        src, dst = (mid_out, mid_in) if kind == 0 else (edge_out.at[kind - 1], edge_in.at[kind - 1])
        return pltpu.make_async_remote_copy(
            src_ref=src.at[d], dst_ref=dst.at[d],
            send_sem=red_send.at[kind, d], recv_sem=red_recv.at[kind, d],
            device_id=peer(d), device_id_type=MESH,
        )

    def send(kind, d):
        @pl.when(d != 0)
        def _():
            red_copy(kind, d).start()

    def mid_sums():
        first, count = halo, own - 2 * halo

        def one(k, carry):
            d = lax.rem(k + 1, events)
            owner = lax.rem(me_e + d, events)
            totals = sums(
                owner, first, count,
                lambda t, f, z: fwd[t, f, z, :, :].astype(jnp.float32)[first:first + count],
            )
            for j in range(share):
                for i in range(3):
                    mid_out[d, i * share + j] = totals[j][i].astype(jnp.bfloat16)
            send(0, d)
            return carry

        lax.fori_loop(0, events, one, 0)

    def edge_sums(side):
        start = 0 if side == 0 else own - halo
        group = 0 if side == 0 else own - 2 * TILE

        def one(k, carry):
            d = lax.rem(k + 1, events)
            owner = lax.rem(me_e + d, events)
            totals = sums(
                owner, start, halo,
                lambda t, f, z: fwd[t, f, z, group:group + 2 * TILE, :].astype(jnp.float32)[
                    start - group:start - group + halo
                ],
            )
            flat = [totals[j][i] for i in range(3) for j in range(share)]
            if len(flat) % 2:
                flat.append(flat[-1])
            for m in range(len(flat) // 2):
                pair = jnp.concatenate(flat[2 * m:2 * m + 2], axis=0)
                edge_out[side, d, m] = pair.astype(jnp.bfloat16)
            send(1 + side, d)
            return carry

        lax.fori_loop(0, events, one, 0)

    def phases(phase, carry):
        side = jnp.where(phase == 1, first_side, 1 - first_side)

        @pl.when(phase > 0)
        def _():
            receive(side)

        advance(phase, side)

        @pl.when(phase == 0)
        def _():
            @pl.when(odd == 1)
            def _():
                pl.semaphore_wait(barrier, events - 1)
                pl.semaphore_signal(all_sem, inc=1, device_id=(me_e, left), device_id_type=MESH)

            @pl.when(odd == 0)
            def _():
                pl.semaphore_wait(all_sem, 1)

            for t in range(steps):
                fwd_copy(t).wait()
            mid_sums()

        for value in range(2):
            @pl.when((phase > 0) & (side == value))
            def _(value=value):
                edge_sums(value)

        return carry

    lax.fori_loop(0, 3, phases, 0)

    def combine(j, start, n, totals):
        k_lame, half_shear, k_dens = totals
        k_shear = 2.0 * half_shear
        z = me_e * share + j
        p, s, d = (x[z, start:start + n, :] for x in (p_raw, s_raw, d_raw))
        lame, shear = d * (p * p - 2.0 * s * s), d * s * s
        out_ref[0, j, start:start + n, :] = 2.0 * d * p * p * k_lame
        out_ref[1, j, start:start + n, :] = 2.0 * d * s * s * (k_shear - 2.0 * k_lame)
        out_ref[2, j, start:start + n, :] = d * k_dens + lame * k_lame + shear * k_shear

    def gathered(out, into, m):
        return out[0, m].astype(jnp.float32) + sum(
            into[d, m].astype(jnp.float32) for d in range(1, events)
        )

    for d in range(1, events):
        red_copy(0, d).wait()
    for j in range(share):
        combine(
            j, halo, own - 2 * halo, [gathered(mid_out, mid_in, i * share + j) for i in range(3)]
        )

    for side in range(2):
        exchange(side).wait_send()

    for side in range(2):
        for d in range(1, events):
            red_copy(1 + side, d).wait()
    for side in range(2):
        start = 0 if side == 0 else own - halo
        tiles = [gathered(edge_out.at[side], edge_in.at[side], m) for m in range(edge_out.shape[2])]
        flat = [t[h * halo:(h + 1) * halo] for t in tiles for h in range(2)]
        for j in range(share):
            combine(j, start, halo, [flat[i * share + j] for i in range(3)])


def shards(adjoint_init, forward_state, p_speed, s_speed, density):
    levels, own, lat = p_speed.shape
    steps = forward_state.shape[1]
    events = lax.axis_size("event")
    share, halo = levels // events, steps
    assert halo == TILE and own % 16 == 0 and own >= 4 * TILE and lax.axis_size("lon") % 2 == 0
    rows = own + 2 * halo
    f32, bf16 = jnp.float32, jnp.bfloat16
    anywhere = pl.BlockSpec(memory_space=pltpu.HBM)
    edge_tiles = (3 * share + 1) // 2
    dma = pltpu.SemaphoreType.DMA
    return pl.pallas_call(
        kernel,
        out_shape=jax.ShapeDtypeStruct((3, share, own, lat), f32),
        in_specs=[anywhere] * 5,
        out_specs=pl.BlockSpec(memory_space=pltpu.VMEM),
        scratch_shapes=[
            pltpu.VMEM(adjoint_init.shape[1:], bf16),
            pltpu.VMEM(forward_state.shape[1:], bf16),
            pltpu.VMEM(p_speed.shape, f32),
            pltpu.VMEM(p_speed.shape, f32),
            pltpu.VMEM(p_speed.shape, f32),
            pltpu.VMEM((steps // 2 + 1, 3, levels + 2, rows, lat), f32),
            pltpu.VMEM((steps // 2, 3, levels + 2, rows, lat), f32),
            pltpu.VMEM((6, levels, rows, lat), f32),
            pltpu.VMEM((6, levels, rows, lat), f32),
            pltpu.VMEM((steps - 1, 6, levels, rows, lat), f32),
            pltpu.VMEM((4, levels, rows, lat), f32),
            pltpu.VMEM((2, 12, levels // 2, 2 * halo, lat), bf16),
            pltpu.VMEM((2, 12, levels // 2, 2 * halo, lat), bf16),
            pltpu.VMEM((events, 3 * share, own - 2 * halo, lat), bf16),
            pltpu.VMEM((events, 3 * share, own - 2 * halo, lat), bf16),
            pltpu.VMEM((2, events, edge_tiles, 2 * halo, lat), bf16),
            pltpu.VMEM((2, events, edge_tiles, 2 * halo, lat), bf16),
            dma((4,)), dma((steps,)), dma((2,)), dma((2,)),
            dma((3, events)), dma((3, events)),
            pltpu.SemaphoreType.REGULAR, pltpu.SemaphoreType.REGULAR,
        ],
        compiler_params=pltpu.CompilerParams(
            collective_id=0, has_side_effects=True, vmem_limit_bytes=60 * 2**20
        ),
        name="adjoint",
    )(adjoint_init, forward_state, p_speed, s_speed, density)


def solution(mesh):
    placed = (
        P("event", None, None, "lon", None),
        P("event", None, None, None, "lon", None),
        P(None, "lon", None),
        P(None, "lon", None),
        P(None, "lon", None),
    )
    return jax.shard_map(
        shards, mesh=mesh, in_specs=placed, out_specs=P(None, "event", "lon", None), check_vma=False
    )
```

```python
import jax
import jax.numpy as jnp
from jax import lax
from jax.experimental import pallas as pl
from jax.experimental.pallas import tpu as pltpu
from jax.sharding import PartitionSpec as P

XX, YY, ZZ, XY, XZ, YZ = range(6)
VX, VY, VZ = range(3)
BUOY, LAME, SHEAR, TWICE = range(4)
TILE = 8
MESH = pl.DeviceIdType.MESH


def behind_lat(a):
    lane = lax.broadcasted_iota(jnp.int32, a.shape, 1)
    return a - jnp.where(lane == 0, 0.0, pltpu.roll(a, 1, 1))


def ahead_lat(a):
    lane = lax.broadcasted_iota(jnp.int32, a.shape, 1)
    last = a.shape[1] - 1
    return jnp.where(lane == last, 0.0, pltpu.roll(a, last, 1)) - a


def kernel(
    adj_hbm, fwd_hbm, p_hbm, s_hbm, d_hbm, out_ref,
    adj, fwd, p_raw, s_raw, d_raw,
    v_even, v_odd, s_even, s_odd, rates, mat,
    halo_out, halo_in, mid_out, mid_in, edge_out, edge_in,
    local_sem, fwd_sem, halo_send, halo_recv, red_send, red_recv, lon_sem, all_sem,
):
    levels, own, lat = p_raw.shape
    steps = fwd.shape[0]
    halo = steps
    events, ring = lax.axis_size("event"), lax.axis_size("lon")
    me_e, me_l = lax.axis_index("event"), lax.axis_index("lon")
    right, left = lax.rem(me_l + 1, ring), lax.rem(me_l + ring - 1, ring)
    share = levels // events
    odd = lax.rem(me_l, 2)
    first_side = 1 - odd

    def peer(d):
        return (lax.rem(me_e + d, events), me_l)

    local = [
        pltpu.make_async_copy(src, dst, local_sem.at[k])
        for k, (src, dst) in enumerate(
            ((adj_hbm.at[0], adj), (d_hbm, d_raw), (p_hbm, p_raw), (s_hbm, s_raw))
        )
    ]
    for copy in local:
        copy.start()

    def fwd_copy(t):
        return pltpu.make_async_copy(fwd_hbm.at[0, t], fwd.at[t], fwd_sem.at[t])

    barrier = pltpu.get_barrier_semaphore()

    @pl.when(odd == 1)
    def _():
        for neighbour in (left, right):
            pl.semaphore_signal(barrier, inc=1, device_id=(me_e, neighbour), device_id_type=MESH)

    zeros = jnp.zeros((own + 2 * halo, lat), jnp.float32)
    for ref, count in ((v_even, steps // 2 + 1), (v_odd, steps // 2)):
        for i in range(count):
            ref[i, VZ, 0] = zeros
            ref[i, VX, levels + 1] = zeros
            ref[i, VY, levels + 1] = zeros

    for copy in local:
        copy.wait()
    for t in range(steps):
        fwd_copy(t).start()

    def prepare(i, carry):
        edges = [[[], []] for _ in range(12)]
        for j in range(2):
            z = 2 * i + j
            d, p, s = d_raw[z], p_raw[z], s_raw[z]
            shear = d * s * s
            rows = [adj[f, z].astype(jnp.float32) for f in range(9)]
            rows += [1.0 / d, d * (p * p - 2.0 * s * s), shear]
            for f in range(3):
                v_even[0, f, z + 1, halo:halo + own, :] = rows[f]
            for f in range(6):
                s_even[f, z, halo:halo + own, :] = rows[3 + f]
            for f in range(3):
                mat[f, z, halo:halo + own, :] = rows[9 + f]
            mat[TWICE, z, halo:halo + own, :] = shear + shear
            for f in range(12):
                edges[f][0].append(rows[f][:halo])
                edges[f][1].append(rows[f][own - halo:])
        for f in range(12):
            for side in range(2):
                pair = jnp.concatenate(edges[f][side], axis=0)
                halo_out[side, f, i] = pair.astype(jnp.bfloat16)
        return carry

    lax.fori_loop(0, levels // 2, prepare, 0)

    def exchange(side):
        return pltpu.make_async_remote_copy(
            src_ref=halo_out.at[side], dst_ref=halo_in.at[side],
            send_sem=halo_send.at[side], recv_sem=halo_recv.at[side],
            device_id=(me_e, jnp.where(side == 0, left, right)), device_id_type=MESH,
        )

    def start_exchange():
        for side in range(2):
            exchange(side).start()

    def answer():
        pl.semaphore_wait(barrier, 2)
        for neighbour in (left, right):
            pl.semaphore_signal(lon_sem, inc=1, device_id=(me_e, neighbour), device_id_type=MESH)
        start_exchange()

    def greet_events():
        pl.semaphore_wait(lon_sem, 2)
        start_exchange()
        for d in range(1, events):
            pl.semaphore_signal(barrier, inc=1, device_id=peer(d), device_id_type=MESH)

    def receive(side):
        source = 1 - side
        exchange(source).wait_recv()
        start = jnp.where(side == 0, 0, halo + own)

        def unpack(i, carry):
            for f in range(12):
                pair = halo_in[source, f, i].astype(jnp.float32)
                for j in range(2):
                    rows = pair[j * halo:(j + 1) * halo]
                    z = 2 * i + j
                    if f < 3:
                        v_even[0, f, z + 1, pl.ds(start, halo), :] = rows
                    elif f < 9:
                        s_even[f - 3, z, pl.ds(start, halo), :] = rows
                    else:
                        mat[f - 9, z, pl.ds(start, halo), :] = rows
                        if f - 9 == SHEAR:
                            mat[TWICE, z, pl.ds(start, halo), :] = rows + rows
            return carry

        lax.fori_loop(0, levels // 2, unpack, 0)

    def velocity(s_ref, v_from, i_from, v_to, i_to, q):
        base = halo + q
        here, back = pl.ds(base, TILE), pl.ds(base - 1, TILE)
        for z in range(levels):
            if z == 0:
                xz_under = yz_under = None
                zz = s_ref[ZZ, 0, here, :]
            xy, xy_back = s_ref[XY, z, here, :], s_ref[XY, z, back, :]
            xz, xz_back = s_ref[XZ, z, here, :], s_ref[XZ, z, back, :]
            yz = s_ref[YZ, z, here, :]
            fx = (s_ref[XX, z, here, :] - s_ref[XX, z, back, :]) + behind_lat(xy_back)
            fy = (xy - xy_back) + ahead_lat(s_ref[YY, z, here, :])
            fz = (xz - xz_back) + behind_lat(yz)
            fx = fx + (xz_back if z == 0 else xz_back - xz_under)
            fy = fy + (yz if z == 0 else yz - yz_under)
            xz_under, yz_under = xz_back, yz
            if z + 1 < levels:
                above = s_ref[ZZ, z + 1, here, :]
                fz = fz + (above - zz)
                zz = above
            else:
                fz = fz - zz
            b, b_back = mat[BUOY, z, here, :], mat[BUOY, z, back, :]
            v_to[i_to, VX, z + 1, back, :] = v_from[i_from, VX, z + 1, back, :] + b_back * fx
            v_to[i_to, VY, z + 1, here, :] = v_from[i_from, VY, z + 1, here, :] + b * fy
            v_to[i_to, VZ, z + 1, here, :] = v_from[i_from, VZ, z + 1, here, :] + b * fz

    def stress(s_from, s_to, v_ref, i_v, e_at, q):
        base = halo + q
        here, back, ahead = (pl.ds(base + k, TILE) for k in (0, -1, 1))
        for z in range(levels):
            if z == 0:
                vx, vy, vz_under = v_ref[i_v, VX, 1, here, :], v_ref[i_v, VY, 1, here, :], None
            vz = v_ref[i_v, VZ, z + 1, here, :]
            exx = vx - v_ref[i_v, VX, z + 1, back, :]
            eyy = behind_lat(vy)
            ezz = vz if z == 0 else vz - vz_under
            gxy = ahead_lat(vx) + (v_ref[i_v, VY, z + 1, ahead, :] - vy)
            gxz = v_ref[i_v, VZ, z + 1, ahead, :] - vz
            gyz = ahead_lat(vz)
            vz_under = vz
            if z + 1 < levels:
                above_x, above_y = v_ref[i_v, VX, z + 2, here, :], v_ref[i_v, VY, z + 2, here, :]
                gxz, gyz = gxz + (above_x - vx), gyz + (above_y - vy)
                vx, vy = above_x, above_y
            else:
                gxz, gyz = gxz - vx, gyz - vy
            for f, e in enumerate((exx, eyy, ezz, gxy, gxz, gyz)):
                rates[e_at, f, z, here, :] = e
            volume = mat[LAME, z, here, :] * (exx + eyy + ezz)
            twice, shear = mat[TWICE, z, here, :], mat[SHEAR, z, here, :]
            for f, e in ((XX, exx), (YY, eyy), (ZZ, ezz)):
                s_to[f, z, here, :] = (s_from[f, z, here, :] + volume) + twice * e
            for f, g in ((XY, gxy), (XZ, gxz), (YZ, gyz)):
                s_to[f, z, here, :] = s_from[f, z, here, :] + shear * g

    def advance(phase, side):
        inner = phase == 0

        def pair(i, carry):
            for parity in range(2):
                t = 2 * i + 1 + parity
                s_from, s_to = (s_even, s_odd) if parity == 0 else (s_odd, s_even)
                v_from, v_to = (v_even, v_odd) if parity == 0 else (v_odd, v_even)

                def v_block(b, carry, s_from=s_from, v_from=v_from, v_to=v_to, t=t, up=parity):
                    edge = jnp.where(side == 0, t - halo, own + 1 - t)
                    q = jnp.where(inner, jnp.minimum(t + TILE * b, own - TILE + 1 - t), edge)
                    velocity(s_from, v_from, i, v_to, i + up, q)
                    return carry

                def s_block(b, carry, s_from=s_from, s_to=s_to, v_to=v_to, t=t, up=parity):
                    edge = jnp.where(side == 0, t - halo, own - t)
                    q = jnp.where(inner, jnp.minimum(t + TILE * b, own - TILE - t), edge)
                    stress(s_from, s_to, v_to, i + up, t - 1, q)
                    return carry

                blocks = jnp.where(inner, (own + 1 - 2 * t + TILE - 1) // TILE, 1)
                lax.fori_loop(0, blocks, v_block, 0)
                blocks = jnp.where(inner, (own - 2 * t + TILE - 1) // TILE, 1)
                blocks = jnp.where(t < steps, blocks, 0)
                lax.fori_loop(0, blocks, s_block, 0)

                @pl.when(inner & (i == 0) & (odd == parity))
                def _(parity=parity):
                    answer() if parity == 0 else greet_events()
            return carry

        lax.fori_loop(0, steps // 2, pair, 0)

    def sums(owner, start, n, rows_of):
        totals = [[None] * 3 for _ in range(share)]
        rows = slice(halo + start, halo + start + n)
        for t in range(1, steps + 1):
            v_ref, i = (v_odd, (t - 1) // 2) if t % 2 else (v_even, t // 2)
            for j in range(share):
                z = owner * share + j

                def v(c, off=0, dz=0):
                    return v_ref[i, c, z + 1 + dz, rows.start + off:rows.stop + off, :]

                F = [rows_of(t - 1, f, z) for f in range(9)]
                if t < steps:
                    vx, vy, vz = v(VX), v(VY), v(VZ)
                    exx, eyy, ezz, gxy, gxz, gyz = (rates[t - 1, f, z, rows, :] for f in range(6))
                else:
                    if j == 0:
                        vx, vy, under = v(VX), v(VY), v(VZ, 0, -1)
                    else:
                        vx, vy, under = above_x, above_y, vz
                    vz, above_x, above_y = v(VZ), v(VX, 0, 1), v(VY, 0, 1)
                    exx = vx - v(VX, -1)
                    eyy = behind_lat(vy)
                    ezz = vz - under
                    gxy = ahead_lat(vx) + (v(VY, 1) - vy)
                    gxz = (above_x - vx) + (v(VZ, 1) - vz)
                    gyz = (above_y - vy) + ahead_lat(vz)
                terms = (
                    (exx + eyy + ezz) * (F[3] + F[4] + F[5]),
                    (exx * F[3] + eyy * F[4] + ezz * F[5]) + (gxy * F[6] + gxz * F[7] + gyz * F[8]),
                    vx * F[0] + vy * F[1] + vz * F[2],
                )
                for k in range(3):
                    old = totals[j][k]
                    totals[j][k] = terms[k] if old is None else old + terms[k]
        return totals

    def red_copy(kind, d):
        src, dst = (mid_out, mid_in) if kind == 0 else (edge_out.at[kind - 1], edge_in.at[kind - 1])
        return pltpu.make_async_remote_copy(
            src_ref=src.at[d], dst_ref=dst.at[d],
            send_sem=red_send.at[kind, d], recv_sem=red_recv.at[kind, d],
            device_id=peer(d), device_id_type=MESH,
        )

    def send(kind, d):
        @pl.when(d != 0)
        def _():
            red_copy(kind, d).start()

    def mid_sums():
        first, count = halo, own - 2 * halo

        def one(k, carry):
            d = lax.rem(k + 1, events)
            owner = lax.rem(me_e + d, events)
            totals = sums(
                owner, first, count,
                lambda t, f, z: fwd[t, f, z, :, :].astype(jnp.float32)[first:first + count],
            )
            for j in range(share):
                for i in range(3):
                    mid_out[d, i * share + j] = totals[j][i].astype(jnp.bfloat16)
            send(0, d)
            return carry

        lax.fori_loop(0, events, one, 0)

    def edge_sums(side):
        start = 0 if side == 0 else own - halo
        group = 0 if side == 0 else own - 2 * TILE

        def one(k, carry):
            d = lax.rem(k + 1, events)
            owner = lax.rem(me_e + d, events)
            totals = sums(
                owner, start, halo,
                lambda t, f, z: fwd[t, f, z, group:group + 2 * TILE, :].astype(jnp.float32)[
                    start - group:start - group + halo
                ],
            )
            flat = [totals[j][i] for i in range(3) for j in range(share)]
            if len(flat) % 2:
                flat.append(flat[-1])
            for m in range(len(flat) // 2):
                pair = jnp.concatenate(flat[2 * m:2 * m + 2], axis=0)
                edge_out[side, d, m] = pair.astype(jnp.bfloat16)
            send(1 + side, d)
            return carry

        lax.fori_loop(0, events, one, 0)

    def phases(phase, carry):
        side = jnp.where(phase == 1, first_side, 1 - first_side)

        @pl.when(phase > 0)
        def _():
            receive(side)

        advance(phase, side)

        @pl.when(phase == 0)
        def _():
            @pl.when(odd == 1)
            def _():
                pl.semaphore_wait(barrier, events - 1)
                pl.semaphore_signal(all_sem, inc=1, device_id=(me_e, left), device_id_type=MESH)

            @pl.when(odd == 0)
            def _():
                pl.semaphore_wait(all_sem, 1)

            for t in range(steps):
                fwd_copy(t).wait()
            mid_sums()

        for value in range(2):
            @pl.when((phase > 0) & (side == value))
            def _(value=value):
                edge_sums(value)

        return carry

    lax.fori_loop(0, 3, phases, 0)

    def combine(j, start, n, totals):
        k_lame, half_shear, k_dens = totals
        k_shear = 2.0 * half_shear
        z = me_e * share + j
        p, s, d = (x[z, start:start + n, :] for x in (p_raw, s_raw, d_raw))
        lame, shear = d * (p * p - 2.0 * s * s), d * s * s
        out_ref[0, j, start:start + n, :] = 2.0 * d * p * p * k_lame
        out_ref[1, j, start:start + n, :] = 2.0 * d * s * s * (k_shear - 2.0 * k_lame)
        out_ref[2, j, start:start + n, :] = d * k_dens + lame * k_lame + shear * k_shear

    def gathered(out, into, m):
        return out[0, m].astype(jnp.float32) + sum(
            into[d, m].astype(jnp.float32) for d in range(1, events)
        )

    for d in range(1, events):
        red_copy(0, d).wait()
    for j in range(share):
        combine(
            j, halo, own - 2 * halo, [gathered(mid_out, mid_in, i * share + j) for i in range(3)]
        )

    for side in range(2):
        exchange(side).wait_send()

    for side in range(2):
        for d in range(1, events):
            red_copy(1 + side, d).wait()
    for side in range(2):
        start = 0 if side == 0 else own - halo
        tiles = [gathered(edge_out.at[side], edge_in.at[side], m) for m in range(edge_out.shape[2])]
        flat = [t[h * halo:(h + 1) * halo] for t in tiles for h in range(2)]
        for j in range(share):
            combine(j, start, halo, [flat[i * share + j] for i in range(3)])


def shards(adjoint_init, forward_state, p_speed, s_speed, density):
    levels, own, lat = p_speed.shape
    steps = forward_state.shape[1]
    events = lax.axis_size("event")
    share, halo = levels // events, steps
    assert halo == TILE and own % 16 == 0 and own >= 4 * TILE and lax.axis_size("lon") % 2 == 0
    rows = own + 2 * halo
    f32, bf16 = jnp.float32, jnp.bfloat16
    anywhere = pl.BlockSpec(memory_space=pltpu.HBM)
    edge_tiles = (3 * share + 1) // 2
    dma = pltpu.SemaphoreType.DMA
    return pl.pallas_call(
        kernel,
        out_shape=pltpu.VMEM((3, share, own, lat), f32),
        in_specs=[anywhere] * 5,
        out_specs=pl.BlockSpec(memory_space=pltpu.VMEM),
        scratch_shapes=[
            pltpu.VMEM(adjoint_init.shape[1:], bf16),
            pltpu.VMEM(forward_state.shape[1:], bf16),
            pltpu.VMEM(p_speed.shape, f32),
            pltpu.VMEM(p_speed.shape, f32),
            pltpu.VMEM(p_speed.shape, f32),
            pltpu.VMEM((steps // 2 + 1, 3, levels + 2, rows, lat), f32),
            pltpu.VMEM((steps // 2, 3, levels + 2, rows, lat), f32),
            pltpu.VMEM((6, levels, rows, lat), f32),
            pltpu.VMEM((6, levels, rows, lat), f32),
            pltpu.VMEM((steps - 1, 6, levels, rows, lat), f32),
            pltpu.VMEM((4, levels, rows, lat), f32),
            pltpu.VMEM((2, 12, levels // 2, 2 * halo, lat), bf16),
            pltpu.VMEM((2, 12, levels // 2, 2 * halo, lat), bf16),
            pltpu.VMEM((events, 3 * share, own - 2 * halo, lat), bf16),
            pltpu.VMEM((events, 3 * share, own - 2 * halo, lat), bf16),
            pltpu.VMEM((2, events, edge_tiles, 2 * halo, lat), bf16),
            pltpu.VMEM((2, events, edge_tiles, 2 * halo, lat), bf16),
            dma((4,)), dma((steps,)), dma((2,)), dma((2,)),
            dma((3, events)), dma((3, events)),
            pltpu.SemaphoreType.REGULAR, pltpu.SemaphoreType.REGULAR,
        ],
        compiler_params=pltpu.CompilerParams(
            collective_id=0, has_side_effects=True, vmem_limit_bytes=60 * 2**20
        ),
        name="adjoint",
    )(adjoint_init, forward_state, p_speed, s_speed, density)


def solution(mesh):
    placed = (
        P("event", None, None, "lon", None),
        P("event", None, None, None, "lon", None),
        P(None, "lon", None),
        P(None, "lon", None),
        P(None, "lon", None),
    )
    return jax.shard_map(
        shards, mesh=mesh, in_specs=placed, out_specs=P(None, "event", "lon", None), check_vma=False
    )
```

```python
import jax
import jax.numpy as jnp
from jax import lax
from jax.experimental import pallas as pl
from jax.experimental.pallas import tpu as pltpu
from jax.sharding import PartitionSpec as P

XX, YY, ZZ, XY, XZ, YZ = range(6)
VX, VY, VZ = range(3)
BUOY, LAME, SHEAR, TWICE = range(4)
TILE = 8
MESH = pl.DeviceIdType.MESH


def behind_lat(a):
    lane = lax.broadcasted_iota(jnp.int32, a.shape, 1)
    return a - jnp.where(lane == 0, 0.0, pltpu.roll(a, 1, 1))


def ahead_lat(a):
    lane = lax.broadcasted_iota(jnp.int32, a.shape, 1)
    last = a.shape[1] - 1
    return jnp.where(lane == last, 0.0, pltpu.roll(a, last, 1)) - a


def kernel(
    adj_hbm, fwd_hbm, p_hbm, s_hbm, d_hbm, out_ref,
    adj, fwd, p_raw, s_raw, d_raw,
    v_even, v_odd, s_even, s_odd, rates, mat,
    halo_out, halo_in, mid_out, mid_in, edge_out, edge_in,
    local_sem, fwd_sem, halo_send, halo_recv, red_send, red_recv, lon_sem, all_sem,
):
    levels, own, lat = p_raw.shape
    steps = fwd.shape[0]
    halo = steps
    events, ring = lax.axis_size("event"), lax.axis_size("lon")
    me_e, me_l = lax.axis_index("event"), lax.axis_index("lon")
    right, left = lax.rem(me_l + 1, ring), lax.rem(me_l + ring - 1, ring)
    share = levels // events
    odd = lax.rem(me_l, 2)
    first_side = 1 - odd

    def partner(d):
        total, bit = 0, 1
        while bit < events:
            mine, other = lax.rem(me_e // bit, 2), lax.rem(d // bit, 2)
            total += bit * (mine + other - 2 * mine * other)
            bit *= 2
        return total

    def peer(d):
        return (partner(jnp.int32(d)), me_l)

    local = [
        pltpu.make_async_copy(src, dst, local_sem.at[k])
        for k, (src, dst) in enumerate(
            ((adj_hbm.at[0], adj), (d_hbm, d_raw), (p_hbm, p_raw), (s_hbm, s_raw))
        )
    ]
    for copy in local:
        copy.start()

    def fwd_copy(t):
        return pltpu.make_async_copy(fwd_hbm.at[0, t], fwd.at[t], fwd_sem.at[t])

    barrier = pltpu.get_barrier_semaphore()

    @pl.when(odd == 1)
    def _():
        for neighbour in (left, right):
            pl.semaphore_signal(barrier, inc=1, device_id=(me_e, neighbour), device_id_type=MESH)

    zeros = jnp.zeros((own + 2 * halo, lat), jnp.float32)
    for ref, count in ((v_even, steps // 2 + 1), (v_odd, steps // 2)):
        for i in range(count):
            ref[i, VZ, 0] = zeros
            ref[i, VX, levels + 1] = zeros
            ref[i, VY, levels + 1] = zeros

    for copy in local:
        copy.wait()
    for t in range(steps):
        fwd_copy(t).start()

    @pl.when(odd == 0)
    def _():
        pl.semaphore_wait(barrier, 2)
        for neighbour in (left, right):
            pl.semaphore_signal(lon_sem, inc=1, device_id=(me_e, neighbour), device_id_type=MESH)

    def prepare(i, carry):
        edges = [[[], []] for _ in range(12)]
        for j in range(2):
            z = 2 * i + j
            d, p, s = d_raw[z], p_raw[z], s_raw[z]
            shear = d * s * s
            rows = [adj[f, z].astype(jnp.float32) for f in range(9)]
            rows += [1.0 / d, d * (p * p - 2.0 * s * s), shear]
            for f in range(3):
                v_even[0, f, z + 1, halo:halo + own, :] = rows[f]
            for f in range(6):
                s_even[f, z, halo:halo + own, :] = rows[3 + f]
            for f in range(3):
                mat[f, z, halo:halo + own, :] = rows[9 + f]
            mat[TWICE, z, halo:halo + own, :] = shear + shear
            for f in range(12):
                edges[f][0].append(rows[f][:halo])
                edges[f][1].append(rows[f][own - halo:])
        for f in range(12):
            for side in range(2):
                pair = jnp.concatenate(edges[f][side], axis=0)
                halo_out[side, f, i] = pair.astype(jnp.bfloat16)
        return carry

    lax.fori_loop(0, levels // 2, prepare, 0)

    def exchange(side):
        return pltpu.make_async_remote_copy(
            src_ref=halo_out.at[side], dst_ref=halo_in.at[side],
            send_sem=halo_send.at[side], recv_sem=halo_recv.at[side],
            device_id=(me_e, jnp.where(side == 0, left, right)), device_id_type=MESH,
        )

    def start_exchange():
        exchange(1 - first_side).start()
        exchange(first_side).start()

    @pl.when(odd == 0)
    def _():
        start_exchange()

    def greet_events():
        pl.semaphore_wait(lon_sem, 2)
        start_exchange()
        for d in range(1, events):
            pl.semaphore_signal(barrier, inc=1, device_id=peer(d), device_id_type=MESH)

    def receive(side):
        source = 1 - side
        exchange(source).wait_recv()
        start = jnp.where(side == 0, 0, halo + own)

        def unpack(i, carry):
            for f in range(12):
                pair = halo_in[source, f, i].astype(jnp.float32)
                for j in range(2):
                    rows = pair[j * halo:(j + 1) * halo]
                    z = 2 * i + j
                    if f < 3:
                        v_even[0, f, z + 1, pl.ds(start, halo), :] = rows
                    elif f < 9:
                        s_even[f - 3, z, pl.ds(start, halo), :] = rows
                    else:
                        mat[f - 9, z, pl.ds(start, halo), :] = rows
                        if f - 9 == SHEAR:
                            mat[TWICE, z, pl.ds(start, halo), :] = rows + rows
            return carry

        lax.fori_loop(0, levels // 2, unpack, 0)

    def velocity(s_ref, v_from, i_from, v_to, i_to, q):
        base = halo + q
        here, back = pl.ds(base, TILE), pl.ds(base - 1, TILE)
        for z in range(levels):
            if z == 0:
                xz_under = yz_under = None
                zz = s_ref[ZZ, 0, here, :]
            xy, xy_back = s_ref[XY, z, here, :], s_ref[XY, z, back, :]
            xz, xz_back = s_ref[XZ, z, here, :], s_ref[XZ, z, back, :]
            yz = s_ref[YZ, z, here, :]
            fx = (s_ref[XX, z, here, :] - s_ref[XX, z, back, :]) + behind_lat(xy_back)
            fy = (xy - xy_back) + ahead_lat(s_ref[YY, z, here, :])
            fz = (xz - xz_back) + behind_lat(yz)
            fx = fx + (xz_back if z == 0 else xz_back - xz_under)
            fy = fy + (yz if z == 0 else yz - yz_under)
            xz_under, yz_under = xz_back, yz
            if z + 1 < levels:
                above = s_ref[ZZ, z + 1, here, :]
                fz = fz + (above - zz)
                zz = above
            else:
                fz = fz - zz
            b, b_back = mat[BUOY, z, here, :], mat[BUOY, z, back, :]
            v_to[i_to, VX, z + 1, back, :] = v_from[i_from, VX, z + 1, back, :] + b_back * fx
            v_to[i_to, VY, z + 1, here, :] = v_from[i_from, VY, z + 1, here, :] + b * fy
            v_to[i_to, VZ, z + 1, here, :] = v_from[i_from, VZ, z + 1, here, :] + b * fz

    def stress(s_from, s_to, v_ref, i_v, e_at, q):
        base = halo + q
        here, back, ahead = (pl.ds(base + k, TILE) for k in (0, -1, 1))
        for z in range(levels):
            if z == 0:
                vx, vy, vz_under = v_ref[i_v, VX, 1, here, :], v_ref[i_v, VY, 1, here, :], None
            vz = v_ref[i_v, VZ, z + 1, here, :]
            exx = vx - v_ref[i_v, VX, z + 1, back, :]
            eyy = behind_lat(vy)
            ezz = vz if z == 0 else vz - vz_under
            gxy = ahead_lat(vx) + (v_ref[i_v, VY, z + 1, ahead, :] - vy)
            gxz = v_ref[i_v, VZ, z + 1, ahead, :] - vz
            gyz = ahead_lat(vz)
            vz_under = vz
            if z + 1 < levels:
                above_x, above_y = v_ref[i_v, VX, z + 2, here, :], v_ref[i_v, VY, z + 2, here, :]
                gxz, gyz = gxz + (above_x - vx), gyz + (above_y - vy)
                vx, vy = above_x, above_y
            else:
                gxz, gyz = gxz - vx, gyz - vy
            for f, e in enumerate((exx, eyy, ezz, gxy, gxz, gyz)):
                rates[e_at, f, z, here, :] = e
            volume = mat[LAME, z, here, :] * (exx + eyy + ezz)
            twice, shear = mat[TWICE, z, here, :], mat[SHEAR, z, here, :]
            for f, e in ((XX, exx), (YY, eyy), (ZZ, ezz)):
                s_to[f, z, here, :] = (s_from[f, z, here, :] + volume) + twice * e
            for f, g in ((XY, gxy), (XZ, gxz), (YZ, gyz)):
                s_to[f, z, here, :] = s_from[f, z, here, :] + shear * g

    def refs(parity):
        stresses, velocities = (s_even, s_odd), (v_even, v_odd)
        return (stresses[parity], stresses[1 - parity], velocities[parity], velocities[1 - parity])

    def inner_pair(first):
        def covers(width):
            return -(-width // TILE)

        def pair(i, carry):
            for parity in range(2):
                t, t_least = 2 * i + 1 + parity, 2 * first + 1 + parity
                s_from, s_to, v_from, v_to = refs(parity)
                at = i + parity
                for b in range(covers(own + 1 - 2 * t_least)):
                    q = jnp.minimum(t + TILE * b, own - TILE + 1 - t)
                    velocity(s_from, v_from, i, v_to, at, q)

                if first == 0 and parity == 0:
                    pl.when((i == 0) & (odd == 1))(greet_events)

                @pl.when(t < steps)
                def _(s_from=s_from, s_to=s_to, v_to=v_to, t=t, at=at, t_least=t_least):
                    for b in range(covers(own - 2 * t_least)):
                        q = jnp.minimum(t + TILE * b, own - TILE - t)
                        stress(s_from, s_to, v_to, at, t - 1, q)

            return carry

        return pair

    def advance_edge(side):
        def pair(i, carry):
            for parity in range(2):
                t = 2 * i + 1 + parity
                s_from, s_to, v_from, v_to = refs(parity)
                at = i + parity
                velocity(s_from, v_from, i, v_to, at, jnp.where(side == 0, t - halo, own + 1 - t))

                @pl.when(t < steps)
                def _(s_from=s_from, s_to=s_to, v_to=v_to, t=t, at=at):
                    q = jnp.where(side == 0, t - halo, own - t)
                    stress(s_from, s_to, v_to, at, t - 1, q)
            return carry

        lax.fori_loop(0, steps // 2, pair, 0)

    def sums(owner, start, n, rows_of):
        totals = [[None] * 3 for _ in range(share)]
        rows = slice(halo + start, halo + start + n)
        for t in range(1, steps + 1):
            v_ref, i = (v_odd, (t - 1) // 2) if t % 2 else (v_even, t // 2)
            for j in range(share):
                z = owner * share + j

                def v(c, off=0, dz=0):
                    return v_ref[i, c, z + 1 + dz, rows.start + off:rows.stop + off, :]

                F = [rows_of(t - 1, f, z) for f in range(9)]
                if t < steps:
                    vx, vy, vz = v(VX), v(VY), v(VZ)
                    exx, eyy, ezz, gxy, gxz, gyz = (rates[t - 1, f, z, rows, :] for f in range(6))
                else:
                    if j == 0:
                        vx, vy, under = v(VX), v(VY), v(VZ, 0, -1)
                    else:
                        vx, vy, under = above_x, above_y, vz
                    vz, above_x, above_y = v(VZ), v(VX, 0, 1), v(VY, 0, 1)
                    exx = vx - v(VX, -1)
                    eyy = behind_lat(vy)
                    ezz = vz - under
                    gxy = ahead_lat(vx) + (v(VY, 1) - vy)
                    gxz = (above_x - vx) + (v(VZ, 1) - vz)
                    gyz = (above_y - vy) + ahead_lat(vz)
                terms = (
                    (exx + eyy + ezz) * (F[3] + F[4] + F[5]),
                    (exx * F[3] + eyy * F[4] + ezz * F[5]) + (gxy * F[6] + gxz * F[7] + gyz * F[8]),
                    vx * F[0] + vy * F[1] + vz * F[2],
                )
                for k in range(3):
                    old = totals[j][k]
                    totals[j][k] = terms[k] if old is None else old + terms[k]
        return totals

    def red_copy(kind, d):
        src, dst = (mid_out, mid_in) if kind == 0 else (edge_out.at[kind - 1], edge_in.at[kind - 1])
        return pltpu.make_async_remote_copy(
            src_ref=src.at[d], dst_ref=dst.at[d],
            send_sem=red_send.at[kind, d], recv_sem=red_recv.at[kind, d],
            device_id=peer(d), device_id_type=MESH,
        )

    def send(kind, d):
        @pl.when(d != 0)
        def _():
            red_copy(kind, d).start()

    far, near = (0, events - 1), (events - 1, events)

    def mid_sums(which):
        first, count = halo, own - 2 * halo

        def one(k, carry):
            d = events - 1 - k
            owner = partner(d)
            totals = sums(
                owner, first, count,
                lambda t, f, z: fwd[t, f, z, :, :].astype(jnp.float32)[first:first + count],
            )
            for j in range(share):
                for i in range(3):
                    mid_out[d, i * share + j] = totals[j][i].astype(jnp.bfloat16)
            send(0, d)
            return carry

        lax.fori_loop(*which, one, 0)

    def edge_sums(side, which):
        start = 0 if side == 0 else own - halo
        group = 0 if side == 0 else own - 2 * TILE

        def one(k, carry):
            d = events - 1 - k
            owner = partner(d)
            totals = sums(
                owner, start, halo,
                lambda t, f, z: fwd[t, f, z, group:group + 2 * TILE, :].astype(jnp.float32)[
                    start - group:start - group + halo
                ],
            )
            flat = [totals[j][i] for i in range(3) for j in range(share)]
            if len(flat) % 2:
                flat.append(flat[-1])
            for m in range(len(flat) // 2):
                pair = jnp.concatenate(flat[2 * m:2 * m + 2], axis=0)
                edge_out[side, d, m] = pair.astype(jnp.bfloat16)
            send(1 + side, d)
            return carry

        lax.fori_loop(*which, one, 0)

    cuts = [0, steps // 4, steps // 2]
    for low, high in zip(cuts, cuts[1:]):
        lax.fori_loop(low, high, inner_pair(low), 0)

    @pl.when(odd == 1)
    def _():
        pl.semaphore_wait(barrier, events - 1)
        pl.semaphore_signal(all_sem, inc=1, device_id=(me_e, left), device_id_type=MESH)

    @pl.when(odd == 0)
    def _():
        pl.semaphore_wait(all_sem, 1)

    for t in range(steps):
        fwd_copy(t).wait()
    mid_sums(far)

    def edges(k, carry):
        side = jnp.where(k == 0, first_side, 1 - first_side)
        receive(side)
        advance_edge(side)
        for value in range(2):
            @pl.when(side == value)
            def _(value=value):
                edge_sums(value, far)

        return carry

    lax.fori_loop(0, 2, edges, 0)

    mid_sums(near)
    for side in range(2):
        edge_sums(side, near)

    def combine(j, start, n, totals):
        k_lame, half_shear, k_dens = totals
        k_shear = 2.0 * half_shear
        z = me_e * share + j
        p, s, d = (x[z, start:start + n, :] for x in (p_raw, s_raw, d_raw))
        lame, shear = d * (p * p - 2.0 * s * s), d * s * s
        out_ref[0, j, start:start + n, :] = 2.0 * d * p * p * k_lame
        out_ref[1, j, start:start + n, :] = 2.0 * d * s * s * (k_shear - 2.0 * k_lame)
        out_ref[2, j, start:start + n, :] = d * k_dens + lame * k_lame + shear * k_shear

    def gathered(out, into, m):
        return out[0, m].astype(jnp.float32) + sum(
            into[d, m].astype(jnp.float32) for d in range(1, events)
        )

    for d in range(1, events):
        red_copy(0, d).wait()
    for j in range(share):
        combine(
            j, halo, own - 2 * halo, [gathered(mid_out, mid_in, i * share + j) for i in range(3)]
        )

    for side in range(2):
        exchange(side).wait_send()

    for side in range(2):
        for d in range(1, events):
            red_copy(1 + side, d).wait()
    for side in range(2):
        start = 0 if side == 0 else own - halo
        tiles = [gathered(edge_out.at[side], edge_in.at[side], m) for m in range(edge_out.shape[2])]
        flat = [t[h * halo:(h + 1) * halo] for t in tiles for h in range(2)]
        for j in range(share):
            combine(j, start, halo, [flat[i * share + j] for i in range(3)])


def shards(adjoint_init, forward_state, p_speed, s_speed, density):
    levels, own, lat = p_speed.shape
    steps = forward_state.shape[1]
    events = lax.axis_size("event")
    share, halo = levels // events, steps
    assert events & (events - 1) == 0
    assert halo == TILE and own % 16 == 0 and own >= 4 * TILE and lax.axis_size("lon") % 2 == 0
    rows = own + 2 * halo
    f32, bf16 = jnp.float32, jnp.bfloat16
    anywhere = pl.BlockSpec(memory_space=pltpu.HBM)
    edge_tiles = (3 * share + 1) // 2
    dma = pltpu.SemaphoreType.DMA
    return pl.pallas_call(
        kernel,
        out_shape=pltpu.VMEM((3, share, own, lat), f32),
        in_specs=[anywhere] * 5,
        out_specs=pl.BlockSpec(memory_space=pltpu.VMEM),
        scratch_shapes=[
            pltpu.VMEM(adjoint_init.shape[1:], bf16),
            pltpu.VMEM(forward_state.shape[1:], bf16),
            pltpu.VMEM(p_speed.shape, f32),
            pltpu.VMEM(p_speed.shape, f32),
            pltpu.VMEM(p_speed.shape, f32),
            pltpu.VMEM((steps // 2 + 1, 3, levels + 2, rows, lat), f32),
            pltpu.VMEM((steps // 2, 3, levels + 2, rows, lat), f32),
            pltpu.VMEM((6, levels, rows, lat), f32),
            pltpu.VMEM((6, levels, rows, lat), f32),
            pltpu.VMEM((steps - 1, 6, levels, rows, lat), f32),
            pltpu.VMEM((4, levels, rows, lat), f32),
            pltpu.VMEM((2, 12, levels // 2, 2 * halo, lat), bf16),
            pltpu.VMEM((2, 12, levels // 2, 2 * halo, lat), bf16),
            pltpu.VMEM((events, 3 * share, own - 2 * halo, lat), bf16),
            pltpu.VMEM((events, 3 * share, own - 2 * halo, lat), bf16),
            pltpu.VMEM((2, events, edge_tiles, 2 * halo, lat), bf16),
            pltpu.VMEM((2, events, edge_tiles, 2 * halo, lat), bf16),
            dma((4,)), dma((steps,)), dma((2,)), dma((2,)),
            dma((3, events)), dma((3, events)),
            pltpu.SemaphoreType.REGULAR, pltpu.SemaphoreType.REGULAR,
        ],
        compiler_params=pltpu.CompilerParams(
            collective_id=0, has_side_effects=True, vmem_limit_bytes=60 * 2**20
        ),
        name="adjoint",
    )(adjoint_init, forward_state, p_speed, s_speed, density)


def solution(mesh):
    placed = (
        P("event", None, None, "lon", None),
        P("event", None, None, None, "lon", None),
        P(None, "lon", None),
        P(None, "lon", None),
        P(None, "lon", None),
    )
    return jax.shard_map(
        shards, mesh=mesh, in_specs=placed, out_specs=P(None, "event", "lon", None), check_vma=False
    )
```

```python
import jax
import jax.numpy as jnp
from jax import lax
from jax.experimental import pallas as pl
from jax.experimental.pallas import tpu as pltpu
from jax.sharding import PartitionSpec as P

XX, YY, ZZ, XY, XZ, YZ = range(6)
VX, VY, VZ = range(3)
BUOY, LAME, SHEAR, TWICE = range(4)
TILE = 8
MESH = pl.DeviceIdType.MESH


def behind_lat(a):
    lane = lax.broadcasted_iota(jnp.int32, a.shape, 1)
    return a - jnp.where(lane == 0, 0.0, pltpu.roll(a, 1, 1))


def ahead_lat(a):
    lane = lax.broadcasted_iota(jnp.int32, a.shape, 1)
    last = a.shape[1] - 1
    return jnp.where(lane == last, 0.0, pltpu.roll(a, last, 1)) - a


def kernel(
    adj_hbm, fwd_hbm, p_hbm, s_hbm, d_hbm, out_ref,
    adj, fwd, p_raw, s_raw, d_raw,
    v_even, v_odd, s_even, s_odd, rates, mat,
    halo_out, halo_in, mid_out, mid_in, edge_out, edge_in,
    local_sem, fwd_sem, halo_send, halo_recv, red_send, red_recv, lon_sem, all_sem,
):
    levels, own, lat = p_raw.shape
    steps = fwd.shape[0]
    halo = steps
    events, ring = lax.axis_size("event"), lax.axis_size("lon")
    me_e, me_l = lax.axis_index("event"), lax.axis_index("lon")
    right, left = lax.rem(me_l + 1, ring), lax.rem(me_l + ring - 1, ring)
    share = levels // events
    odd = lax.rem(me_l, 2)
    first_side = 1 - odd

    def partner(d):
        total, bit = 0, 1
        while bit < events:
            mine, other = lax.rem(me_e // bit, 2), lax.rem(d // bit, 2)
            total += bit * (mine + other - 2 * mine * other)
            bit *= 2
        return total

    def peer(d):
        return (partner(jnp.int32(d)), me_l)

    half = levels // 2

    def local_copies(part):
        z = pl.ds(part * half, half)
        pairs = (
            (adj_hbm.at[0, :, z], adj.at[:, z]), (d_hbm.at[z], d_raw.at[z]),
            (p_hbm.at[z], p_raw.at[z]), (s_hbm.at[z], s_raw.at[z]),
        )
        return [
            pltpu.make_async_copy(src, dst, local_sem.at[part, k])
            for k, (src, dst) in enumerate(pairs)
        ]

    for part in range(2):
        for copy in local_copies(part):
            copy.start()

    def fwd_copy(t):
        return pltpu.make_async_copy(fwd_hbm.at[0, t], fwd.at[t], fwd_sem.at[t])

    barrier = pltpu.get_barrier_semaphore()

    @pl.when(odd == 1)
    def _():
        for neighbour in (left, right):
            pl.semaphore_signal(barrier, inc=1, device_id=(me_e, neighbour), device_id_type=MESH)

    zeros = jnp.zeros((own + 2 * halo, lat), jnp.float32)
    for ref, count in ((v_even, steps // 2 + 1), (v_odd, steps // 2)):
        for i in range(count):
            ref[i, VZ, 0] = zeros
            ref[i, VX, levels + 1] = zeros
            ref[i, VY, levels + 1] = zeros

    for copy in local_copies(0):
        copy.wait()

    @pl.when(odd == 0)
    def _():
        pl.semaphore_wait(barrier, 2)
        for neighbour in (left, right):
            pl.semaphore_signal(lon_sem, inc=1, device_id=(me_e, neighbour), device_id_type=MESH)

    def prepare(i, carry):
        edges = [[[], []] for _ in range(12)]
        for j in range(2):
            z = 2 * i + j
            d, p, s = d_raw[z], p_raw[z], s_raw[z]
            shear = d * s * s
            rows = [adj[f, z].astype(jnp.float32) for f in range(9)]
            rows += [1.0 / d, d * (p * p - 2.0 * s * s), shear]
            for f in range(3):
                v_even[0, f, z + 1, halo:halo + own, :] = rows[f]
            for f in range(6):
                s_even[f, z, halo:halo + own, :] = rows[3 + f]
            for f in range(3):
                mat[f, z, halo:halo + own, :] = rows[9 + f]
            mat[TWICE, z, halo:halo + own, :] = shear + shear
            for f in range(12):
                edges[f][0].append(rows[f][:halo])
                edges[f][1].append(rows[f][own - halo:])
        for f in range(12):
            for side in range(2):
                pair = jnp.concatenate(edges[f][side], axis=0)
                halo_out[side, f, i] = pair.astype(jnp.bfloat16)
        return carry

    lax.fori_loop(0, half // 2, prepare, 0)
    for copy in local_copies(1):
        copy.wait()
    for t in range(steps):
        fwd_copy(t).start()
    lax.fori_loop(half // 2, half, prepare, 0)

    def exchange(side):
        return pltpu.make_async_remote_copy(
            src_ref=halo_out.at[side], dst_ref=halo_in.at[side],
            send_sem=halo_send.at[side], recv_sem=halo_recv.at[side],
            device_id=(me_e, jnp.where(side == 0, left, right)), device_id_type=MESH,
        )

    def start_exchange():
        exchange(1 - first_side).start()
        exchange(first_side).start()

    @pl.when(odd == 0)
    def _():
        start_exchange()

    def greet_events():
        pl.semaphore_wait(lon_sem, 2)
        start_exchange()
        for d in range(1, events):
            pl.semaphore_signal(barrier, inc=1, device_id=peer(d), device_id_type=MESH)

    def receive(side):
        source = 1 - side
        exchange(source).wait_recv()
        start = jnp.where(side == 0, 0, halo + own)

        def unpack(i, carry):
            for f in range(12):
                pair = halo_in[source, f, i].astype(jnp.float32)
                for j in range(2):
                    rows = pair[j * halo:(j + 1) * halo]
                    z = 2 * i + j
                    if f < 3:
                        v_even[0, f, z + 1, pl.ds(start, halo), :] = rows
                    elif f < 9:
                        s_even[f - 3, z, pl.ds(start, halo), :] = rows
                    else:
                        mat[f - 9, z, pl.ds(start, halo), :] = rows
                        if f - 9 == SHEAR:
                            mat[TWICE, z, pl.ds(start, halo), :] = rows + rows
            return carry

        lax.fori_loop(0, levels // 2, unpack, 0)

    def velocity(s_ref, v_from, i_from, v_to, i_to, q):
        base = halo + q
        here, back = pl.ds(base, TILE), pl.ds(base - 1, TILE)
        for z in range(levels):
            if z == 0:
                xz_under = yz_under = None
                zz = s_ref[ZZ, 0, here, :]
            xy, xy_back = s_ref[XY, z, here, :], s_ref[XY, z, back, :]
            xz, xz_back = s_ref[XZ, z, here, :], s_ref[XZ, z, back, :]
            yz = s_ref[YZ, z, here, :]
            fx = (s_ref[XX, z, here, :] - s_ref[XX, z, back, :]) + behind_lat(xy_back)
            fy = (xy - xy_back) + ahead_lat(s_ref[YY, z, here, :])
            fz = (xz - xz_back) + behind_lat(yz)
            fx = fx + (xz_back if z == 0 else xz_back - xz_under)
            fy = fy + (yz if z == 0 else yz - yz_under)
            xz_under, yz_under = xz_back, yz
            if z + 1 < levels:
                above = s_ref[ZZ, z + 1, here, :]
                fz = fz + (above - zz)
                zz = above
            else:
                fz = fz - zz
            b, b_back = mat[BUOY, z, here, :], mat[BUOY, z, back, :]
            v_to[i_to, VX, z + 1, back, :] = v_from[i_from, VX, z + 1, back, :] + b_back * fx
            v_to[i_to, VY, z + 1, here, :] = v_from[i_from, VY, z + 1, here, :] + b * fy
            v_to[i_to, VZ, z + 1, here, :] = v_from[i_from, VZ, z + 1, here, :] + b * fz

    def stress(s_from, s_to, v_ref, i_v, e_at, q):
        base = halo + q
        here, back, ahead = (pl.ds(base + k, TILE) for k in (0, -1, 1))
        for z in range(levels):
            if z == 0:
                vx, vy, vz_under = v_ref[i_v, VX, 1, here, :], v_ref[i_v, VY, 1, here, :], None
            vz = v_ref[i_v, VZ, z + 1, here, :]
            exx = vx - v_ref[i_v, VX, z + 1, back, :]
            eyy = behind_lat(vy)
            ezz = vz if z == 0 else vz - vz_under
            gxy = ahead_lat(vx) + (v_ref[i_v, VY, z + 1, ahead, :] - vy)
            gxz = v_ref[i_v, VZ, z + 1, ahead, :] - vz
            gyz = ahead_lat(vz)
            vz_under = vz
            if z + 1 < levels:
                above_x, above_y = v_ref[i_v, VX, z + 2, here, :], v_ref[i_v, VY, z + 2, here, :]
                gxz, gyz = gxz + (above_x - vx), gyz + (above_y - vy)
                vx, vy = above_x, above_y
            else:
                gxz, gyz = gxz - vx, gyz - vy
            for f, e in enumerate((exx, eyy, ezz, gxy, gxz, gyz)):
                rates[e_at, f, z, here, :] = e
            volume = mat[LAME, z, here, :] * (exx + eyy + ezz)
            twice, shear = mat[TWICE, z, here, :], mat[SHEAR, z, here, :]
            for f, e in ((XX, exx), (YY, eyy), (ZZ, ezz)):
                s_to[f, z, here, :] = (s_from[f, z, here, :] + volume) + twice * e
            for f, g in ((XY, gxy), (XZ, gxz), (YZ, gyz)):
                s_to[f, z, here, :] = s_from[f, z, here, :] + shear * g

    def refs(parity):
        stresses, velocities = (s_even, s_odd), (v_even, v_odd)
        return (stresses[parity], stresses[1 - parity], velocities[parity], velocities[1 - parity])

    def inner_pair(first):
        def covers(width):
            return -(-width // TILE)

        def pair(i, carry):
            for parity in range(2):
                t, t_least = 2 * i + 1 + parity, 2 * first + 1 + parity
                s_from, s_to, v_from, v_to = refs(parity)
                at = i + parity
                for b in range(covers(own + 1 - 2 * t_least)):
                    q = jnp.minimum(t + TILE * b, own - TILE + 1 - t)
                    velocity(s_from, v_from, i, v_to, at, q)

                if first == 0 and parity == 0:
                    pl.when((i == 0) & (odd == 1))(greet_events)

                @pl.when(t < steps)
                def _(s_from=s_from, s_to=s_to, v_to=v_to, t=t, at=at, t_least=t_least):
                    for b in range(covers(own - 2 * t_least)):
                        q = jnp.minimum(t + TILE * b, own - TILE - t)
                        stress(s_from, s_to, v_to, at, t - 1, q)

            return carry

        return pair

    def advance_edge(side):
        def pair(i, carry):
            for parity in range(2):
                t = 2 * i + 1 + parity
                s_from, s_to, v_from, v_to = refs(parity)
                at = i + parity
                velocity(s_from, v_from, i, v_to, at, jnp.where(side == 0, t - halo, own + 1 - t))

                @pl.when(t < steps)
                def _(s_from=s_from, s_to=s_to, v_to=v_to, t=t, at=at):
                    q = jnp.where(side == 0, t - halo, own - t)
                    stress(s_from, s_to, v_to, at, t - 1, q)
            return carry

        lax.fori_loop(0, steps // 2, pair, 0)

    def sums(owner, start, n, rows_of):
        totals = [[None] * 3 for _ in range(share)]
        rows = slice(halo + start, halo + start + n)
        for t in range(1, steps + 1):
            v_ref, i = (v_odd, (t - 1) // 2) if t % 2 else (v_even, t // 2)
            for j in range(share):
                z = owner * share + j

                def v(c, off=0, dz=0):
                    return v_ref[i, c, z + 1 + dz, rows.start + off:rows.stop + off, :]

                F = [rows_of(t - 1, f, z) for f in range(9)]
                if t < steps:
                    vx, vy, vz = v(VX), v(VY), v(VZ)
                    exx, eyy, ezz, gxy, gxz, gyz = (rates[t - 1, f, z, rows, :] for f in range(6))
                else:
                    if j == 0:
                        vx, vy, under = v(VX), v(VY), v(VZ, 0, -1)
                    else:
                        vx, vy, under = above_x, above_y, vz
                    vz, above_x, above_y = v(VZ), v(VX, 0, 1), v(VY, 0, 1)
                    exx = vx - v(VX, -1)
                    eyy = behind_lat(vy)
                    ezz = vz - under
                    gxy = ahead_lat(vx) + (v(VY, 1) - vy)
                    gxz = (above_x - vx) + (v(VZ, 1) - vz)
                    gyz = (above_y - vy) + ahead_lat(vz)
                terms = (
                    (exx + eyy + ezz) * (F[3] + F[4] + F[5]),
                    (exx * F[3] + eyy * F[4] + ezz * F[5]) + (gxy * F[6] + gxz * F[7] + gyz * F[8]),
                    vx * F[0] + vy * F[1] + vz * F[2],
                )
                for k in range(3):
                    old = totals[j][k]
                    totals[j][k] = terms[k] if old is None else old + terms[k]
        return totals

    def red_copy(kind, d):
        src, dst = (mid_out, mid_in) if kind == 0 else (edge_out.at[kind - 1], edge_in.at[kind - 1])
        return pltpu.make_async_remote_copy(
            src_ref=src.at[d], dst_ref=dst.at[d],
            send_sem=red_send.at[kind, d], recv_sem=red_recv.at[kind, d],
            device_id=peer(d), device_id_type=MESH,
        )

    def send(kind, d):
        @pl.when(d != 0)
        def _():
            red_copy(kind, d).start()

    far, near = (0, events - 1), (events - 1, events)

    def mid_sums(which):
        first, count = halo, own - 2 * halo

        def one(k, carry):
            d = events - 1 - k
            owner = partner(d)
            totals = sums(
                owner, first, count,
                lambda t, f, z: fwd[t, f, z, :, :].astype(jnp.float32)[first:first + count],
            )
            for j in range(share):
                for i in range(3):
                    mid_out[d, i * share + j] = totals[j][i].astype(jnp.bfloat16)
            if which == far:
                @pl.when((k == 0) & (odd == 0))
                def _():
                    pl.semaphore_wait(all_sem, 1)

            send(0, d)
            return carry

        lax.fori_loop(*which, one, 0)

    def edge_sums(side, which):
        start = 0 if side == 0 else own - halo
        group = 0 if side == 0 else own - 2 * TILE

        def one(k, carry):
            d = events - 1 - k
            owner = partner(d)
            totals = sums(
                owner, start, halo,
                lambda t, f, z: fwd[t, f, z, group:group + 2 * TILE, :].astype(jnp.float32)[
                    start - group:start - group + halo
                ],
            )
            flat = [totals[j][i] for i in range(3) for j in range(share)]
            if len(flat) % 2:
                flat.append(flat[-1])
            for m in range(len(flat) // 2):
                pair = jnp.concatenate(flat[2 * m:2 * m + 2], axis=0)
                edge_out[side, d, m] = pair.astype(jnp.bfloat16)
            send(1 + side, d)
            return carry

        lax.fori_loop(*which, one, 0)

    cuts = [0, steps // 4, steps // 2]
    for low, high in zip(cuts, cuts[1:]):
        lax.fori_loop(low, high, inner_pair(low), 0)

    @pl.when(odd == 1)
    def _():
        pl.semaphore_wait(barrier, events - 1)
        pl.semaphore_signal(all_sem, inc=1, device_id=(me_e, left), device_id_type=MESH)

    for t in range(steps):
        fwd_copy(t).wait()
    mid_sums(far)

    def edges(k, carry):
        side = jnp.where(k == 0, first_side, 1 - first_side)
        receive(side)
        advance_edge(side)
        for value in range(2):
            @pl.when(side == value)
            def _(value=value):
                edge_sums(value, far)

        return carry

    lax.fori_loop(0, 2, edges, 0)

    mid_sums(near)
    for side in range(2):
        edge_sums(side, near)

    def combine(j, start, n, totals):
        k_lame, half_shear, k_dens = totals
        k_shear = 2.0 * half_shear
        z = me_e * share + j
        p, s, d = (x[z, start:start + n, :] for x in (p_raw, s_raw, d_raw))
        lame, shear = d * (p * p - 2.0 * s * s), d * s * s
        out_ref[0, j, start:start + n, :] = 2.0 * d * p * p * k_lame
        out_ref[1, j, start:start + n, :] = 2.0 * d * s * s * (k_shear - 2.0 * k_lame)
        out_ref[2, j, start:start + n, :] = d * k_dens + lame * k_lame + shear * k_shear

    def gathered(out, into, m):
        return out[0, m].astype(jnp.float32) + sum(
            into[d, m].astype(jnp.float32) for d in range(1, events)
        )

    for d in range(1, events):
        red_copy(0, d).wait()
    for j in range(share):
        combine(
            j, halo, own - 2 * halo, [gathered(mid_out, mid_in, i * share + j) for i in range(3)]
        )

    for side in range(2):
        exchange(side).wait_send()

    for side in range(2):
        for d in range(1, events):
            red_copy(1 + side, d).wait()
    for side in range(2):
        start = 0 if side == 0 else own - halo
        tiles = [gathered(edge_out.at[side], edge_in.at[side], m) for m in range(edge_out.shape[2])]
        flat = [t[h * halo:(h + 1) * halo] for t in tiles for h in range(2)]
        for j in range(share):
            combine(j, start, halo, [flat[i * share + j] for i in range(3)])


def shards(adjoint_init, forward_state, p_speed, s_speed, density):
    levels, own, lat = p_speed.shape
    steps = forward_state.shape[1]
    events = lax.axis_size("event")
    share, halo = levels // events, steps
    assert events & (events - 1) == 0
    assert halo == TILE and own % 16 == 0 and own >= 4 * TILE and lax.axis_size("lon") % 2 == 0
    rows = own + 2 * halo
    f32, bf16 = jnp.float32, jnp.bfloat16
    anywhere = pl.BlockSpec(memory_space=pltpu.HBM)
    edge_tiles = (3 * share + 1) // 2
    dma = pltpu.SemaphoreType.DMA
    return pl.pallas_call(
        kernel,
        out_shape=pltpu.VMEM((3, share, own, lat), f32),
        in_specs=[anywhere] * 5,
        out_specs=pl.BlockSpec(memory_space=pltpu.VMEM),
        scratch_shapes=[
            pltpu.VMEM(adjoint_init.shape[1:], bf16),
            pltpu.VMEM(forward_state.shape[1:], bf16),
            pltpu.VMEM(p_speed.shape, f32),
            pltpu.VMEM(p_speed.shape, f32),
            pltpu.VMEM(p_speed.shape, f32),
            pltpu.VMEM((steps // 2 + 1, 3, levels + 2, rows, lat), f32),
            pltpu.VMEM((steps // 2, 3, levels + 2, rows, lat), f32),
            pltpu.VMEM((6, levels, rows, lat), f32),
            pltpu.VMEM((6, levels, rows, lat), f32),
            pltpu.VMEM((steps - 1, 6, levels, rows, lat), f32),
            pltpu.VMEM((4, levels, rows, lat), f32),
            pltpu.VMEM((2, 12, levels // 2, 2 * halo, lat), bf16),
            pltpu.VMEM((2, 12, levels // 2, 2 * halo, lat), bf16),
            pltpu.VMEM((events, 3 * share, own - 2 * halo, lat), bf16),
            pltpu.VMEM((events, 3 * share, own - 2 * halo, lat), bf16),
            pltpu.VMEM((2, events, edge_tiles, 2 * halo, lat), bf16),
            pltpu.VMEM((2, events, edge_tiles, 2 * halo, lat), bf16),
            dma((2, 4)), dma((steps,)), dma((2,)), dma((2,)),
            dma((3, events)), dma((3, events)),
            pltpu.SemaphoreType.REGULAR, pltpu.SemaphoreType.REGULAR,
        ],
        compiler_params=pltpu.CompilerParams(
            collective_id=0, has_side_effects=True, vmem_limit_bytes=60 * 2**20
        ),
        name="adjoint",
    )(adjoint_init, forward_state, p_speed, s_speed, density)


def solution(mesh):
    placed = (
        P("event", None, None, "lon", None),
        P("event", None, None, None, "lon", None),
        P(None, "lon", None),
        P(None, "lon", None),
        P(None, "lon", None),
    )
    return jax.shard_map(
        shards, mesh=mesh, in_specs=placed, out_specs=P(None, "event", "lon", None), check_vma=False
    )
```

```python
import jax
import jax.numpy as jnp
from jax import lax
from jax.experimental import pallas as pl
from jax.experimental.pallas import tpu as pltpu
from jax.sharding import PartitionSpec as P

XX, YY, ZZ, XY, XZ, YZ = range(6)
VX, VY, VZ = range(3)
BUOY, LAME, SHEAR = range(3)
TILE = 8
MESH = pl.DeviceIdType.MESH


def behind_lat(a):
    lane = lax.broadcasted_iota(jnp.int32, a.shape, 1)
    return a - jnp.where(lane == 0, 0.0, pltpu.roll(a, 1, 1))


def ahead_lat(a):
    lane = lax.broadcasted_iota(jnp.int32, a.shape, 1)
    last = a.shape[1] - 1
    return jnp.where(lane == last, 0.0, pltpu.roll(a, last, 1)) - a


def kernel(
    adj_hbm, fwd_hbm, p_hbm, s_hbm, d_hbm, out_ref,
    adj, fwd, p_raw, s_raw, d_raw,
    v_even, v_odd, s_even, s_odd, rates, mat,
    halo_out, halo_in, mid_out, mid_in, edge_out, edge_in,
    local_sem, fwd_sem, halo_send, halo_recv, red_send, red_recv, lon_sem, all_sem,
):
    levels, own, lat = p_raw.shape
    steps = fwd.shape[0]
    halo = steps
    events, ring = lax.axis_size("event"), lax.axis_size("lon")
    me_e, me_l = lax.axis_index("event"), lax.axis_index("lon")
    right, left = lax.rem(me_l + 1, ring), lax.rem(me_l + ring - 1, ring)
    share = levels // events
    odd = lax.rem(me_l, 2)
    first_side = 1 - odd

    def partner(d):
        total, bit = 0, 1
        while bit < events:
            mine, other = lax.rem(me_e // bit, 2), lax.rem(d // bit, 2)
            total += bit * (mine + other - 2 * mine * other)
            bit *= 2
        return total

    def peer(d):
        return (partner(jnp.int32(d)), me_l)

    half = levels // 2

    def local_copies(part):
        z = pl.ds(part * half, half)
        pairs = (
            (adj_hbm.at[0, :, z], adj.at[:, z]), (d_hbm.at[z], d_raw.at[z]),
            (p_hbm.at[z], p_raw.at[z]), (s_hbm.at[z], s_raw.at[z]),
        )
        return [
            pltpu.make_async_copy(src, dst, local_sem.at[part, k])
            for k, (src, dst) in enumerate(pairs)
        ]

    for part in range(2):
        for copy in local_copies(part):
            copy.start()

    def fwd_copy(t):
        return pltpu.make_async_copy(fwd_hbm.at[0, t], fwd.at[t], fwd_sem.at[t])

    barrier = pltpu.get_barrier_semaphore()

    @pl.when(odd == 1)
    def _():
        for neighbour in (left, right):
            pl.semaphore_signal(barrier, inc=1, device_id=(me_e, neighbour), device_id_type=MESH)

    zeros = jnp.zeros((own + 2 * halo, lat), jnp.float32)
    for ref, count in ((v_even, steps // 2 + 1), (v_odd, steps // 2)):
        for i in range(count):
            ref[i, VZ, 0] = zeros
            ref[i, VX, levels + 1] = zeros
            ref[i, VY, levels + 1] = zeros

    for copy in local_copies(0):
        copy.wait()

    @pl.when(odd == 0)
    def _():
        pl.semaphore_wait(barrier, 2)
        for neighbour in (left, right):
            pl.semaphore_signal(lon_sem, inc=1, device_id=(me_e, neighbour), device_id_type=MESH)

    def prepare(i, carry):
        edges = [[[], []] for _ in range(12)]
        for j in range(2):
            z = 2 * i + j
            d, p, s = d_raw[z], p_raw[z], s_raw[z]
            shear = d * s * s
            rows = [adj[f, z].astype(jnp.float32) for f in range(9)]
            rows += [1.0 / d, d * (p * p - 2.0 * s * s), shear]
            for f in range(3):
                v_even[0, f, z + 1, halo:halo + own, :] = rows[f]
            for f in range(6):
                s_even[f, z, halo:halo + own, :] = rows[3 + f]
            for f in range(3):
                mat[f, z, halo:halo + own, :] = rows[9 + f]
            for f in range(12):
                edges[f][0].append(rows[f][:halo])
                edges[f][1].append(rows[f][own - halo:])
        for f in range(12):
            for side in range(2):
                pair = jnp.concatenate(edges[f][side], axis=0)
                halo_out[side, f, i] = pair.astype(jnp.bfloat16)
        return carry

    lax.fori_loop(0, half // 2, prepare, 0)
    for copy in local_copies(1):
        copy.wait()
    for t in range(steps):
        fwd_copy(t).start()
    lax.fori_loop(half // 2, half, prepare, 0)

    def exchange(side):
        return pltpu.make_async_remote_copy(
            src_ref=halo_out.at[side], dst_ref=halo_in.at[side],
            send_sem=halo_send.at[side], recv_sem=halo_recv.at[side],
            device_id=(me_e, jnp.where(side == 0, left, right)), device_id_type=MESH,
        )

    def start_exchange():
        exchange(1 - first_side).start()
        exchange(first_side).start()

    @pl.when(odd == 0)
    def _():
        start_exchange()

    def greet_events():
        pl.semaphore_wait(lon_sem, 2)
        start_exchange()
        for d in range(1, events):
            pl.semaphore_signal(barrier, inc=1, device_id=peer(d), device_id_type=MESH)

    def receive(side):
        source = 1 - side
        exchange(source).wait_recv()
        start = jnp.where(side == 0, 0, halo + own)

        def unpack(i, carry):
            for f in range(12):
                pair = halo_in[source, f, i].astype(jnp.float32)
                for j in range(2):
                    rows = pair[j * halo:(j + 1) * halo]
                    z = 2 * i + j
                    if f < 3:
                        v_even[0, f, z + 1, pl.ds(start, halo), :] = rows
                    elif f < 9:
                        s_even[f - 3, z, pl.ds(start, halo), :] = rows
                    else:
                        mat[f - 9, z, pl.ds(start, halo), :] = rows
            return carry

        lax.fori_loop(0, levels // 2, unpack, 0)

    def velocity(s_ref, v_from, i_from, v_to, i_to, q):
        base = halo + q
        here, back = pl.ds(base, TILE), pl.ds(base - 1, TILE)
        for z in range(levels):
            if z == 0:
                xz_under = yz_under = None
                zz = s_ref[ZZ, 0, here, :]
            xy, xy_back = s_ref[XY, z, here, :], s_ref[XY, z, back, :]
            xz, xz_back = s_ref[XZ, z, here, :], s_ref[XZ, z, back, :]
            yz = s_ref[YZ, z, here, :]
            fx = (s_ref[XX, z, here, :] - s_ref[XX, z, back, :]) + behind_lat(xy_back)
            fy = (xy - xy_back) + ahead_lat(s_ref[YY, z, here, :])
            fz = (xz - xz_back) + behind_lat(yz)
            fx = fx + (xz_back if z == 0 else xz_back - xz_under)
            fy = fy + (yz if z == 0 else yz - yz_under)
            xz_under, yz_under = xz_back, yz
            if z + 1 < levels:
                above = s_ref[ZZ, z + 1, here, :]
                fz = fz + (above - zz)
                zz = above
            else:
                fz = fz - zz
            b, b_back = mat[BUOY, z, here, :], mat[BUOY, z, back, :]
            v_to[i_to, VX, z + 1, back, :] = v_from[i_from, VX, z + 1, back, :] + b_back * fx
            v_to[i_to, VY, z + 1, here, :] = v_from[i_from, VY, z + 1, here, :] + b * fy
            v_to[i_to, VZ, z + 1, here, :] = v_from[i_from, VZ, z + 1, here, :] + b * fz

    def stress(s_from, s_to, v_ref, i_v, e_at, q):
        base = halo + q
        here, back, ahead = (pl.ds(base + k, TILE) for k in (0, -1, 1))
        for z in range(levels):
            if z == 0:
                vx, vy, vz_under = v_ref[i_v, VX, 1, here, :], v_ref[i_v, VY, 1, here, :], None
            vz = v_ref[i_v, VZ, z + 1, here, :]
            exx = vx - v_ref[i_v, VX, z + 1, back, :]
            eyy = behind_lat(vy)
            ezz = vz if z == 0 else vz - vz_under
            gxy = ahead_lat(vx) + (v_ref[i_v, VY, z + 1, ahead, :] - vy)
            gxz = v_ref[i_v, VZ, z + 1, ahead, :] - vz
            gyz = ahead_lat(vz)
            vz_under = vz
            if z + 1 < levels:
                above_x, above_y = v_ref[i_v, VX, z + 2, here, :], v_ref[i_v, VY, z + 2, here, :]
                gxz, gyz = gxz + (above_x - vx), gyz + (above_y - vy)
                vx, vy = above_x, above_y
            else:
                gxz, gyz = gxz - vx, gyz - vy
            for f, e in enumerate((exx, eyy, ezz, gxy, gxz, gyz)):
                rates[e_at, f, z, here, :] = e
            volume = mat[LAME, z, here, :] * (exx + eyy + ezz)
            shear = mat[SHEAR, z, here, :]
            twice = shear + shear
            for f, e in ((XX, exx), (YY, eyy), (ZZ, ezz)):
                s_to[f, z, here, :] = (s_from[f, z, here, :] + volume) + twice * e
            for f, g in ((XY, gxy), (XZ, gxz), (YZ, gyz)):
                s_to[f, z, here, :] = s_from[f, z, here, :] + shear * g

    def refs(parity):
        stresses, velocities = (s_even, s_odd), (v_even, v_odd)
        return (stresses[parity], stresses[1 - parity], velocities[parity], velocities[1 - parity])

    def inner_pair(first):
        def covers(width):
            return -(-width // TILE)

        def pair(i, carry):
            for parity in range(2):
                t, t_least = 2 * i + 1 + parity, 2 * first + 1 + parity
                s_from, s_to, v_from, v_to = refs(parity)
                at = i + parity
                for b in range(covers(own + 1 - 2 * t_least)):
                    q = jnp.minimum(t + TILE * b, own - TILE + 1 - t)
                    velocity(s_from, v_from, i, v_to, at, q)

                if first == 0 and parity == 0:
                    pl.when((i == 0) & (odd == 1))(greet_events)

                @pl.when(t < steps)
                def _(s_from=s_from, s_to=s_to, v_to=v_to, t=t, at=at, t_least=t_least):
                    for b in range(covers(own - 2 * t_least)):
                        q = jnp.minimum(t + TILE * b, own - TILE - t)
                        stress(s_from, s_to, v_to, at, t - 1, q)

            return carry

        return pair

    def advance_edge(side):
        def pair(i, carry):
            for parity in range(2):
                t = 2 * i + 1 + parity
                s_from, s_to, v_from, v_to = refs(parity)
                at = i + parity
                velocity(s_from, v_from, i, v_to, at, jnp.where(side == 0, t - halo, own + 1 - t))

                @pl.when(t < steps)
                def _(s_from=s_from, s_to=s_to, v_to=v_to, t=t, at=at):
                    q = jnp.where(side == 0, t - halo, own - t)
                    stress(s_from, s_to, v_to, at, t - 1, q)
            return carry

        lax.fori_loop(0, steps // 2, pair, 0)

    def sums(owner, start, n, rows_of):
        totals = [[None] * 3 for _ in range(share)]
        rows = slice(halo + start, halo + start + n)
        for t in range(1, steps + 1):
            v_ref, i = (v_odd, (t - 1) // 2) if t % 2 else (v_even, t // 2)
            for j in range(share):
                z = owner * share + j

                def v(c, off=0, dz=0):
                    return v_ref[i, c, z + 1 + dz, rows.start + off:rows.stop + off, :]

                F = [rows_of(t - 1, f, z) for f in range(9)]
                if t < steps:
                    vx, vy, vz = v(VX), v(VY), v(VZ)
                    exx, eyy, ezz, gxy, gxz, gyz = (rates[t - 1, f, z, rows, :] for f in range(6))
                else:
                    if j == 0:
                        vx, vy, under = v(VX), v(VY), v(VZ, 0, -1)
                    else:
                        vx, vy, under = above_x, above_y, vz
                    vz, above_x, above_y = v(VZ), v(VX, 0, 1), v(VY, 0, 1)
                    exx = vx - v(VX, -1)
                    eyy = behind_lat(vy)
                    ezz = vz - under
                    gxy = ahead_lat(vx) + (v(VY, 1) - vy)
                    gxz = (above_x - vx) + (v(VZ, 1) - vz)
                    gyz = (above_y - vy) + ahead_lat(vz)
                terms = (
                    (exx + eyy + ezz) * (F[3] + F[4] + F[5]),
                    (exx * F[3] + eyy * F[4] + ezz * F[5]) + (gxy * F[6] + gxz * F[7] + gyz * F[8]),
                    vx * F[0] + vy * F[1] + vz * F[2],
                )
                for k in range(3):
                    old = totals[j][k]
                    totals[j][k] = terms[k] if old is None else old + terms[k]
        return totals

    def red_copy(kind, d):
        src, dst = (mid_out, mid_in) if kind == 0 else (edge_out.at[kind - 1], edge_in.at[kind - 1])
        return pltpu.make_async_remote_copy(
            src_ref=src.at[d], dst_ref=dst.at[d],
            send_sem=red_send.at[kind, d], recv_sem=red_recv.at[kind, d],
            device_id=peer(d), device_id_type=MESH,
        )

    def send(kind, d):
        @pl.when(d != 0)
        def _():
            red_copy(kind, d).start()

    far, near = (0, events - 1), (events - 1, events)

    def mid_sums(which):
        first, count = halo, own - 2 * halo

        def one(k, carry):
            d = events - 1 - k
            owner = partner(d)
            totals = sums(
                owner, first, count,
                lambda t, f, z: fwd[t, f, z, :, :].astype(jnp.float32)[first:first + count],
            )
            for j in range(share):
                for i in range(3):
                    mid_out[d, i * share + j] = totals[j][i].astype(jnp.bfloat16)
            if which == far:
                @pl.when((k == 0) & (odd == 0))
                def _():
                    pl.semaphore_wait(all_sem, 1)

            send(0, d)
            return carry

        lax.fori_loop(*which, one, 0)

    def edge_sums(side, which):
        start = 0 if side == 0 else own - halo
        group = 0 if side == 0 else own - 2 * TILE

        def one(k, carry):
            d = events - 1 - k
            owner = partner(d)
            totals = sums(
                owner, start, halo,
                lambda t, f, z: fwd[t, f, z, group:group + 2 * TILE, :].astype(jnp.float32)[
                    start - group:start - group + halo
                ],
            )
            flat = [totals[j][i] for i in range(3) for j in range(share)]
            if len(flat) % 2:
                flat.append(flat[-1])
            for m in range(len(flat) // 2):
                pair = jnp.concatenate(flat[2 * m:2 * m + 2], axis=0)
                edge_out[side, d, m] = pair.astype(jnp.bfloat16)
            send(1 + side, d)
            return carry

        lax.fori_loop(*which, one, 0)

    cuts = [0, steps // 4, steps // 2]
    for low, high in zip(cuts, cuts[1:]):
        lax.fori_loop(low, high, inner_pair(low), 0)

    @pl.when(odd == 1)
    def _():
        pl.semaphore_wait(barrier, events - 1)
        pl.semaphore_signal(all_sem, inc=1, device_id=(me_e, left), device_id_type=MESH)

    for t in range(steps):
        fwd_copy(t).wait()
    mid_sums(far)

    def edges(k, carry):
        side = jnp.where(k == 0, first_side, 1 - first_side)
        receive(side)
        advance_edge(side)
        for value in range(2):
            @pl.when(side == value)
            def _(value=value):
                edge_sums(value, far)

        return carry

    lax.fori_loop(0, 2, edges, 0)

    mid_sums(near)
    for side in range(2):
        edge_sums(side, near)

    def combine(j, start, n, totals):
        k_lame, half_shear, k_dens = totals
        k_shear = 2.0 * half_shear
        z = me_e * share + j
        p, s, d = (x[z, start:start + n, :] for x in (p_raw, s_raw, d_raw))
        lame, shear = d * (p * p - 2.0 * s * s), d * s * s
        out_ref[0, j, start:start + n, :] = 2.0 * d * p * p * k_lame
        out_ref[1, j, start:start + n, :] = 2.0 * d * s * s * (k_shear - 2.0 * k_lame)
        out_ref[2, j, start:start + n, :] = d * k_dens + lame * k_lame + shear * k_shear

    def gathered(out, into, m):
        return out[0, m].astype(jnp.float32) + sum(
            into[d, m].astype(jnp.float32) for d in range(1, events)
        )

    for d in range(1, events):
        red_copy(0, d).wait()
    for j in range(share):
        combine(
            j, halo, own - 2 * halo, [gathered(mid_out, mid_in, i * share + j) for i in range(3)]
        )

    for side in range(2):
        exchange(side).wait_send()

    for side in range(2):
        for d in range(1, events):
            red_copy(1 + side, d).wait()
    for side in range(2):
        start = 0 if side == 0 else own - halo
        tiles = [gathered(edge_out.at[side], edge_in.at[side], m) for m in range(edge_out.shape[2])]
        flat = [t[h * halo:(h + 1) * halo] for t in tiles for h in range(2)]
        for j in range(share):
            combine(j, start, halo, [flat[i * share + j] for i in range(3)])


def shards(adjoint_init, forward_state, p_speed, s_speed, density):
    levels, own, lat = p_speed.shape
    steps = forward_state.shape[1]
    events = lax.axis_size("event")
    share, halo = levels // events, steps
    assert events & (events - 1) == 0
    assert halo == TILE and own % 16 == 0 and own >= 4 * TILE and lax.axis_size("lon") % 2 == 0
    rows = own + 2 * halo
    f32, bf16 = jnp.float32, jnp.bfloat16
    anywhere = pl.BlockSpec(memory_space=pltpu.HBM)
    edge_tiles = (3 * share + 1) // 2
    dma = pltpu.SemaphoreType.DMA
    return pl.pallas_call(
        kernel,
        out_shape=pltpu.VMEM((3, share, own, lat), f32),
        in_specs=[anywhere] * 5,
        out_specs=pl.BlockSpec(memory_space=pltpu.VMEM),
        scratch_shapes=[
            pltpu.VMEM(adjoint_init.shape[1:], bf16),
            pltpu.VMEM(forward_state.shape[1:], bf16),
            pltpu.VMEM(p_speed.shape, f32),
            pltpu.VMEM(p_speed.shape, f32),
            pltpu.VMEM(p_speed.shape, f32),
            pltpu.VMEM((steps // 2 + 1, 3, levels + 2, rows, lat), f32),
            pltpu.VMEM((steps // 2, 3, levels + 2, rows, lat), f32),
            pltpu.VMEM((6, levels, rows, lat), f32),
            pltpu.VMEM((6, levels, rows, lat), f32),
            pltpu.VMEM((steps - 1, 6, levels, rows, lat), f32),
            pltpu.VMEM((3, levels, rows, lat), f32),
            pltpu.VMEM((2, 12, levels // 2, 2 * halo, lat), bf16),
            pltpu.VMEM((2, 12, levels // 2, 2 * halo, lat), bf16),
            pltpu.VMEM((events, 3 * share, own - 2 * halo, lat), bf16),
            pltpu.VMEM((events, 3 * share, own - 2 * halo, lat), bf16),
            pltpu.VMEM((2, events, edge_tiles, 2 * halo, lat), bf16),
            pltpu.VMEM((2, events, edge_tiles, 2 * halo, lat), bf16),
            dma((2, 4)), dma((steps,)), dma((2,)), dma((2,)),
            dma((3, events)), dma((3, events)),
            pltpu.SemaphoreType.REGULAR, pltpu.SemaphoreType.REGULAR,
        ],
        compiler_params=pltpu.CompilerParams(
            collective_id=0, has_side_effects=True, vmem_limit_bytes=60 * 2**20
        ),
        name="adjoint",
    )(adjoint_init, forward_state, p_speed, s_speed, density)


def solution(mesh):
    placed = (
        P("event", None, None, "lon", None),
        P("event", None, None, None, "lon", None),
        P(None, "lon", None),
        P(None, "lon", None),
        P(None, "lon", None),
    )
    return jax.shard_map(
        shards, mesh=mesh, in_specs=placed, out_specs=P(None, "event", "lon", None), check_vma=False
    )
```
